128 devices in a mesh: dp: 32 (over x, z, core), mp: 4 (over y).
Axes of the slice: x: 4, y: 4, z: 4, core: 2. Of those that a mesh axis runs over, the one named last changes fastest.
Arguments:
- queries: bfloat16 [4096, 4, 2560], P('dp', None, 'mp'), may hold values from -96 to 96
- new_keys: bfloat16 [4096, 4, 512], P('dp', None, 'mp'), may hold values from -4 to 4
- new_values: bfloat16 [4096, 4, 512], P('dp', None, 'mp'), may hold values from -12 to 12
- key_cache: bfloat16 [4096, 256, 512], P('dp', None, 'mp'), may hold values from -4 to 4
- value_cache: bfloat16 [4096, 256, 512], P('dp', None, 'mp'), may hold values from -12 to 12
- lengths: int32 [4096], P('dp'), may hold values from 1 to 256
- rewards: int32 [4096], P('dp'), may hold values from 0 to 4
- group_ids: int32 [4096], P('dp'), may hold values from 0 to 511, as said below
- destination: int32 [4096], P('dp'), may hold values from 0 to 4095, as said below
- out_proj: bfloat16 [5120, 2560], P('dp', 'mp'), may hold values from -0.125 to 0.125
- cotangent: bfloat16 [16384, 5120], P('dp', 'mp'), may hold values from -6 to 6
Outputs:
- out_y: bfloat16 [16384, 5120], P('dp', 'mp')
- grad_attn: bfloat16 [16384, 2560], P('dp', 'mp')
- grad_proj: bfloat16 [5120, 2560], P('dp', 'mp')
The draws below stay inside these ranges and needn't reach their ends.
Inputs may be any that keep to these rules, and one draw needn't show every extreme that they name: `group_ids`: each group has exactly 8 responses. `destination`: a permutation of the 4096 positions; positions d * 128 to (d + 1) * 128 - 1 form block d; of the responses of one index of dp at most 8 go to any one block, and exactly 8 to some block.
All inputs are finite; a program needn't handle non-finite values.
Results may differ from the reference program's by a relative error of at most 0.015.
Values may be sent and summed in bfloat16 or wider, within the bound.
No kernel may reach another device: no remote copies, remote signals or barrier semaphores. Data moves between devices by JAX's collectives and lax.ppermute only.
A program may use at most 128 MiB of HBM per device.

```python
import jax
import jax.numpy as jnp
from jax import lax

D = 5120
HD = 128
QH = 20
KVH = 4
ROWS = 128
L = 256
STEPS = 4
G = 8
ROWS_ALL = 4096
GROUPS = 512
TOKENS = 16384
CAP = 8
N_DP = 32


def shared_keys(key):
    drawn = jax.random.normal(jax.random.fold_in(key, 11), (ROWS_ALL, STEPS, KVH * HD), jnp.float32)
    return jnp.clip(drawn, -4.0, 4.0)


def draw_new_keys(key, part):
    return shared_keys(key).astype(jnp.bfloat16)


def draw_queries(key, part):
    drawn = jnp.clip(jax.random.normal(jax.random.fold_in(key, 14), (ROWS_ALL, STEPS, QH * HD), jnp.float32), -4.0, 4.0)
    return drawn.astype(jnp.bfloat16)


def draw_key_cache(key, part):
    drawn = jnp.clip(jax.random.normal(jax.random.fold_in(key, 15), (ROWS_ALL, L, KVH * HD), jnp.float32), -4.0, 4.0)
    return drawn.astype(jnp.bfloat16)


def draw_group_ids(key, part):
    return (jax.random.permutation(jax.random.fold_in(key, 21), ROWS_ALL) // G).astype(jnp.int32)


def draw_destination(key, part):
    slot_total = N_DP * CAP
    owners = jnp.repeat(jnp.arange(N_DP, dtype=jnp.int32), CAP)
    heavy_bin = N_DP // 2
    slot_scores = jax.random.permutation(jax.random.fold_in(key, 32), slot_total).astype(jnp.int32)
    slot_scores = jnp.where(owners == heavy_bin, slot_total + slot_scores, slot_scores)
    ranking = jnp.argsort(slot_scores)
    slot_rank = jnp.zeros((slot_total,), jnp.int32).at[ranking].set(jnp.arange(slot_total, dtype=jnp.int32))
    picked = slot_rank < ROWS - CAP
    device_ids = jnp.arange(N_DP, dtype=jnp.int32)
    counts = jnp.sum(((owners[:, None] == device_ids[None, :]) & picked[:, None]).astype(jnp.int32), axis=0)
    counts = counts + CAP * (device_ids == heavy_bin).astype(jnp.int32)
    traffic = counts[(device_ids[None, :] - device_ids[:, None]) % N_DP]
    offset = jnp.cumsum(traffic, axis=0) - traffic
    begins = jnp.cumsum(traffic, axis=1) - traffic
    shuffle_key = jax.random.fold_in(key, 33)

    def one_source(source):
        targets = jnp.repeat(device_ids, traffic[source], total_repeat_length=ROWS)
        within_rank = jnp.arange(ROWS, dtype=jnp.int32) - begins[source, targets]
        places = targets * ROWS + offset[source, targets] + within_rank
        shuffle = jax.random.permutation(jax.random.fold_in(shuffle_key, source), ROWS)
        return places[shuffle]
    return jax.vmap(one_source)(device_ids).reshape(ROWS_ALL).astype(jnp.int32)


def plant(entries, rng, least, largest):
    longest = entries.shape.index(max(entries.shape))
    spots = []
    for shift in (0, 1):
        where = [jax.random.randint(jax.random.fold_in(rng, axis), (), 0, length) for axis, length in enumerate(entries.shape)]
        where[longest] = (where[longest] + shift) % entries.shape[longest]
        spots.append(tuple(where))
    return entries.at[spots[0]].set(least).at[spots[1]].set(largest)


def with_spikes(values, stream_key, source, target, parts, factor):
    def block_of(dim):
        return (jnp.arange(values.shape[dim]) // (values.shape[dim] // parts)).reshape((-1,) + (1,) * (values.ndim - 1 - dim))

    one_side = jax.random.permutation(stream_key, parts)[block_of(target)]
    second = (block_of(target) + parts // 2) % parts
    return jnp.where((block_of(source) == one_side) | (block_of(source) == second), factor * values, values)


def shard_levels(own_key, dims, split, low, largest):
    gain = 1.0
    for dim, parts in split:
        heights = jax.random.uniform(jax.random.fold_in(jax.random.fold_in(own_key, 6), dim), (parts,), jnp.float32, low / len(split), largest / len(split))
        gain = gain * jnp.repeat(jnp.exp(heights), dims[dim] // parts).reshape((-1,) + (1,) * (len(dims) - 1 - dim))
    return gain


def centred(own_key, extent, width, most, pieces=(), kind=jnp.bfloat16):
    values = width * jax.random.normal(own_key, extent, jnp.float32)
    if pieces:
        values = values * shard_levels(own_key, extent, pieces, -0.22, 0.18)
    return jnp.clip(values, -most, most).astype(kind)


def heavy_noise(rng, shape, width, most, shards, heavy, kind=jnp.bfloat16):
    result = width * jax.random.normal(rng, shape, jnp.float32)
    if shards:
        result = result * shard_levels(rng, shape, shards, -0.22, 0.18)
    return jnp.clip(with_spikes(result, jax.random.fold_in(rng, 3), *heavy), -most, most).astype(kind)


def setup_inputs(seed: int = 0) -> dict:
    keys = jax.random.split(jax.random.key(seed), 12)
    return {
        "queries": draw_queries(jax.random.fold_in(keys[11], 71), 0),
        "new_keys": draw_new_keys(jax.random.fold_in(keys[11], 71), 0),
        "new_values": centred(keys[2], (ROWS_ALL, STEPS, KVH * HD), 2.0, 12.0, ((0, 32), (2, 4))),
        "key_cache": draw_key_cache(jax.random.fold_in(keys[11], 71), 0),
        "value_cache": centred(keys[4], (ROWS_ALL, L, KVH * HD), 2.0, 12.0, ((0, 32), (2, 4))),
        "lengths": plant(jax.random.randint(keys[5], (ROWS_ALL,), 1, L + 1), jax.random.fold_in(keys[5], 1), 1, L).astype(jnp.int32),
        "rewards": plant(jax.random.randint(keys[6], (ROWS_ALL,), 0, 5), jax.random.fold_in(keys[6], 1), 0, 4).astype(jnp.int32),
        "group_ids": draw_group_ids(jax.random.fold_in(keys[11], 71), 0),
        "destination": draw_destination(jax.random.fold_in(keys[11], 71), 0),
        "out_proj": centred(keys[9], (D, QH * HD), (QH * HD) ** -0.5, 0.125, ((0, 32), (1, 4))),
        "cotangent": heavy_noise(keys[10], (TOKENS, D), 1.0, 6.0, ((0, 32), (1, 4)), (0, 1, 32, 2.75)),
    }


def attend(queries, new_keys, new_values, key_cache, value_cache, lengths):
    row_count, step_count, feat_width = queries.shape
    cache_len = key_cache.shape[1]
    kv_heads = key_cache.shape[2] // HD
    per_group = feat_width // HD // kv_heads
    query_heads = queries.astype(jnp.float32).reshape(row_count, step_count, kv_heads, per_group, HD)
    cache_keys = key_cache.astype(jnp.float32).reshape(row_count, cache_len, kv_heads, HD)
    cache_vals = value_cache.astype(jnp.float32).reshape(row_count, cache_len, kv_heads, HD)
    fresh_keys = new_keys.astype(jnp.float32).reshape(row_count, step_count, kv_heads, HD)
    fresh_vals = new_values.astype(jnp.float32).reshape(row_count, step_count, kv_heads, HD)
    score_scale = HD ** (-0.5)
    past_scores = jnp.einsum('rtkgd,rpkd->rtkgp', query_heads, cache_keys) * score_scale
    new_scores = jnp.einsum('rtkgd,rskd->rtkgs', query_heads, fresh_keys) * score_scale
    in_cache = (jnp.arange(cache_len, dtype=jnp.int32)[None, :] < lengths[:, None])[:, None, None, None, :]
    causal = (jnp.arange(step_count, dtype=jnp.int32)[None, :] <= jnp.arange(step_count, dtype=jnp.int32)[:, None])[None, :, None, None, :]
    past_scores = jnp.where(in_cache, past_scores, -jnp.inf)
    new_scores = jnp.where(causal, new_scores, -jnp.inf)
    row_top = jnp.maximum(lax.optimization_barrier(jnp.max(past_scores, axis=-1)), lax.optimization_barrier(jnp.max(new_scores, axis=-1)))[..., None]
    past_exp = jnp.exp(past_scores - row_top)
    new_exp = jnp.exp(new_scores - row_top)
    denominator = lax.optimization_barrier(jnp.sum(past_exp, axis=-1, keepdims=True)) + lax.optimization_barrier(jnp.sum(new_exp, axis=-1, keepdims=True))
    past_weights = lax.optimization_barrier((past_exp / denominator).astype(jnp.bfloat16)).astype(jnp.float32)
    new_weights = lax.optimization_barrier((new_exp / denominator).astype(jnp.bfloat16)).astype(jnp.float32)
    attended = jnp.einsum('rtkgp,rpkd->rtkgd', past_weights, cache_vals) + jnp.einsum('rtkgs,rskd->rtkgd', new_weights, fresh_vals)
    return attended.astype(jnp.bfloat16).reshape(row_count, step_count, feat_width)

def by_device(array):
    return array.reshape((N_DP, ROWS) + array.shape[1:])

def run_block(block_parts):
    return attend(block_parts[0], block_parts[1], block_parts[2], block_parts[3], block_parts[4], block_parts[5])

def add_partial(running, block_parts):
    partial_value = jnp.dot(block_parts[0].T, block_parts[1], preferred_element_type=jnp.float32)
    rounded = lax.optimization_barrier(partial_value.astype(jnp.bfloat16)).astype(jnp.float32)
    return (running + rounded, None)

def reference(queries, new_keys, new_values, key_cache, value_cache, lengths, rewards, group_ids, destination, out_proj, cotangent):
    attention = lax.map(run_block, (by_device(queries), by_device(new_keys), by_device(new_values), by_device(key_cache), by_device(value_cache), by_device(lengths)))
    attention = attention.reshape(ROWS_ALL, STEPS, QH * HD)
    reward_values = rewards.astype(jnp.float32)
    totals = jax.ops.segment_sum(reward_values, group_ids, num_segments=GROUPS)
    squares = jax.ops.segment_sum(reward_values * reward_values, group_ids, num_segments=GROUPS)
    centre = totals[group_ids] / G
    spread = squares[group_ids] / G - centre * centre
    advantage = (reward_values - centre) / jnp.sqrt(jnp.maximum(spread, 1.0))
    moved = jnp.zeros_like(attention).at[destination].set(attention)
    moved_advantage = jnp.zeros((ROWS_ALL,), jnp.float32).at[destination].set(advantage)
    activations = moved.reshape(TOKENS, QH * HD)
    out_y = jnp.dot(activations, out_proj.T, preferred_element_type=jnp.float32).astype(jnp.bfloat16)
    token_advantage = jnp.repeat(moved_advantage, STEPS, total_repeat_length=TOKENS)
    signal = (token_advantage[:, None] * cotangent.astype(jnp.float32)).astype(jnp.bfloat16)
    grad_attn = jnp.dot(signal, out_proj, preferred_element_type=jnp.float32).astype(jnp.bfloat16)
    starting = jnp.zeros((D, QH * HD), jnp.float32)
    summed = lax.scan(add_partial, starting, (signal.reshape(N_DP, ROWS * STEPS, D), activations.reshape(N_DP, ROWS * STEPS, QH * HD)))[0]
    grad_proj = (summed / N_DP).astype(jnp.bfloat16)
    return (out_y, grad_attn, grad_proj)
```

```python
import jax
import jax.numpy as jnp
from jax import lax
from jax.experimental import pallas as pl
from jax.experimental.pallas import tpu as pltpu
from jax.sharding import PartitionSpec as P

HD = 128
G = 8
CAP = 8
NX, NZ, NY = 4, 4, 4
BF = jnp.bfloat16
F32 = jnp.float32


def place(x, z, c):
    return (x % NX) * 8 + (z % NZ) * 2 + c


def everywhere():
    return [(x, z, c) for x in range(NX) for z in range(NZ) for c in range(2)]


def along_x(value, shift):
    return lax.ppermute(
        value, "dp", [(place(x, z, c), place(x + shift, z, c)) for x, z, c in everywhere()]
    )


def along_z(value, shift):
    return lax.ppermute(
        value, "dp", [(place(x, z, c), place(x, z + shift, c)) for x, z, c in everywhere()]
    )


def along_y(value, shift):
    return lax.ppermute(value, "mp", [(y, (y + shift) % NY) for y in range(NY)])


def to_partner(value):
    return lax.ppermute(value, "dp", [(d, d ^ 1) for d in range(32)])


def swap_xy(value):
    pairs = [
        (place(x, z, c) * NY + y, place(y, z, c) * NY + x)
        for x, z, c in everywhere()
        for y in range(NY)
    ]
    return lax.ppermute(value, ("dp", "mp"), pairs)


def attend(queries, new_keys, new_values, key_cache, value_cache, lengths):
    row_count, step_count, feat_width = queries.shape
    cache_len = key_cache.shape[1]
    kv_heads = key_cache.shape[2] // HD
    per_group = feat_width // HD // kv_heads
    query_heads = queries.reshape(row_count, step_count, kv_heads, per_group, HD)
    cache_keys = key_cache.reshape(row_count, cache_len, kv_heads, HD)
    cache_vals = value_cache.reshape(row_count, cache_len, kv_heads, HD)
    fresh_keys = new_keys.reshape(row_count, step_count, kv_heads, HD)
    fresh_vals = new_values.reshape(row_count, step_count, kv_heads, HD)
    score_scale = HD ** (-0.5)
    past_scores = (
        jnp.einsum("rtkgd,rpkd->rtkgp", query_heads, cache_keys, preferred_element_type=jnp.float32)
        * score_scale
    )
    new_scores = (
        jnp.einsum("rtkgd,rskd->rtkgs", query_heads, fresh_keys, preferred_element_type=jnp.float32)
        * score_scale
    )
    in_cache = (jnp.arange(cache_len, dtype=jnp.int32)[None, :] < lengths[:, None])[
        :, None, None, None, :
    ]
    causal = (
        jnp.arange(step_count, dtype=jnp.int32)[None, :]
        <= jnp.arange(step_count, dtype=jnp.int32)[:, None]
    )[None, :, None, None, :]
    past_scores = jnp.where(in_cache, past_scores, -jnp.inf)
    new_scores = jnp.where(causal, new_scores, -jnp.inf)
    row_top = jnp.maximum(jnp.max(past_scores, axis=-1), jnp.max(new_scores, axis=-1))[..., None]
    past_exp = jnp.exp(past_scores - row_top)
    new_exp = jnp.exp(new_scores - row_top)
    denominator = jnp.sum(past_exp, axis=-1, keepdims=True) + jnp.sum(
        new_exp, axis=-1, keepdims=True
    )
    past_weights = (past_exp / denominator).astype(jnp.bfloat16)
    new_weights = (new_exp / denominator).astype(jnp.bfloat16)
    attended = jnp.einsum(
        "rtkgp,rpkd->rtkgd", past_weights, cache_vals, preferred_element_type=jnp.float32
    )
    attended = attended + jnp.einsum(
        "rtkgs,rskd->rtkgd", new_weights, fresh_vals, preferred_element_type=jnp.float32
    )
    return attended.astype(jnp.bfloat16).reshape(row_count * step_count, feat_width)


def meta_kernel(block_ref, words_ref, adv_ref, slot_ref):
    rows = words_ref.shape[1]
    first = block_ref[0] * rows
    wanted = first + lax.broadcasted_iota(jnp.int32, (rows, rows), 0)
    found = jnp.zeros((rows, rows), jnp.int32)
    for k in range(words_ref.shape[0]):
        word = words_ref[k : k + 1, :]
        found = found + jnp.where((word & 4095) == wanted, word, 0)
    found = jnp.sum(found, axis=1, keepdims=True)
    group = (found >> 12) & 511
    sums = jnp.zeros((rows, rows), jnp.int32)
    for k in range(words_ref.shape[0]):
        word = words_ref[k : k + 1, :]
        reward = (word >> 21) & 7
        sums = sums + jnp.where(((word >> 12) & 511) == group, reward + reward * reward * 4096, 0)
    sums = jnp.sum(sums, axis=1, keepdims=True)
    centre = (sums & 4095).astype(F32) / G
    spread = (sums >> 12).astype(F32) / G - centre * centre
    reward = ((found >> 21) & 7).astype(F32)
    adv_ref[...] = (reward - centre) / jnp.sqrt(jnp.maximum(spread, 1.0))
    slot_ref[...] = (found >> 24) & 255


def meta(block, words):
    rows = words.shape[1]
    return pl.pallas_call(
        meta_kernel,
        out_shape=(
            jax.ShapeDtypeStruct((rows, 1), F32),
            jax.ShapeDtypeStruct((rows, 1), jnp.int32),
        ),
        in_specs=[
            pl.BlockSpec(memory_space=pltpu.SMEM),
            pl.BlockSpec(memory_space=pltpu.VMEM),
        ],
        out_specs=(
            pl.BlockSpec(memory_space=pltpu.VMEM),
            pl.BlockSpec(memory_space=pltpu.VMEM),
        ),
        name="meta",
    )(block, words)


def grad_kernel(where_ref, left_ref, *refs):
    mine, theirs, (a_ref, b_ref) = refs[:4], refs[4:8], refs[8:]
    tokens = mine[0].shape[0]
    x, z, y = where_ref[0], where_ref[1], where_ref[2]
    half = left_ref.shape[0] // 2
    step = half // NZ
    for i in range(NY):
        xs = lax.rem(y - i - x + 2 * NX, NX)
        left = left_ref[...]
        got = jnp.dot(left[:, :tokens], mine[i][...], preferred_element_type=F32)
        got = got + jnp.dot(left[:, tokens:], theirs[i][...], preferred_element_type=F32)
        got = got.astype(BF)
        for k in range(NZ):
            zs = lax.rem(k - z + NZ, NZ)
            a_ref[xs, zs] = got[k * step : (k + 1) * step]
            b_ref[zs, xs] = got[half + k * step : half + (k + 1) * step]


def grad_parts(where, left, mine, theirs):
    width = mine[0].shape[1]
    step = left.shape[0] // 2 // NZ
    shape = jax.ShapeDtypeStruct((4, 4, step, width), BF)
    return pl.pallas_call(
        grad_kernel,
        out_shape=(shape, shape),
        in_specs=[pl.BlockSpec(memory_space=pltpu.SMEM)]
        + [pl.BlockSpec(memory_space=pltpu.VMEM)] * 9,
        out_specs=(
            pl.BlockSpec(memory_space=pltpu.VMEM),
            pl.BlockSpec(memory_space=pltpu.VMEM),
        ),
        name="grad_parts",
    )(where, left, *mine, *theirs)


def total(*parts):
    result = parts[0].astype(F32)
    for part in parts[1:]:
        result = result + part.astype(F32)
    return result


def local(
    queries,
    new_keys,
    new_values,
    key_cache,
    value_cache,
    lengths,
    rewards,
    group_ids,
    destination,
    out_proj,
    cotangent,
):
    row_count, step_count, feat_width = queries.shape
    tokens = row_count * step_count
    block = lax.axis_index("dp").astype(jnp.int32)
    y = lax.axis_index("mp").astype(jnp.int32)
    x, z, c = block // 8, (block // 2) % 4, block % 2

    weight_tile = swap_xy(out_proj)

    target = destination // row_count
    positions = jnp.arange(row_count, dtype=jnp.int32)
    earlier = (target[:, None] == target[None, :]) & (positions[None, :] < positions[:, None])
    rank = jnp.sum(earlier.astype(jnp.int32), axis=1)
    words = destination | (group_ids << 12) | (rewards << 21) | ((block * CAP + rank) << 24)
    words = words[None, :]
    words = jnp.concatenate([words, to_partner(words)], axis=0)
    words = jnp.concatenate([words] + [along_z(words, s) for s in (1, 3, 2)], axis=0)
    words = jnp.concatenate([words] + [along_x(words, s) for s in (1, 3, 2)], axis=0)
    advantage, from_slot = meta(block[None], words)

    weight = lax.all_gather(weight_tile, "dp", axis=0, tiled=True)
    weight = weight.reshape(NX, -1, feat_width)

    token_advantage = jnp.broadcast_to(advantage[:, None, :], (row_count, step_count, 1))
    signal = (token_advantage.reshape(tokens, 1) * cotangent.astype(F32)).astype(BF)
    turned = signal.T.reshape(NZ, 2, 2, -1, tokens)
    sides = jnp.transpose(turned, (1, 2, 0, 3, 4)).reshape(2, -1, tokens)
    own_side = lax.dynamic_index_in_dim(sides, c, 0, keepdims=False)
    other_side = lax.dynamic_index_in_dim(sides, 1 - c, 0, keepdims=False)
    left = jnp.concatenate([own_side, to_partner(other_side)], axis=1)

    attention = attend(queries, new_keys, new_values, key_cache, value_cache, lengths)

    slots = 32 * CAP
    steps = jnp.arange(step_count, dtype=jnp.int32)
    goes_to = ((target * CAP + rank)[:, None] * step_count + steps[None, :]).reshape(1, tokens)
    spread_out = (
        lax.broadcasted_iota(jnp.int32, (slots * step_count, tokens), 0) == goes_to
    ).astype(BF)
    send_rows = jnp.dot(spread_out, attention, preferred_element_type=F32).astype(BF)
    got_rows = lax.all_to_all(send_rows, "dp", split_axis=0, concat_axis=0, tiled=True)
    comes_from = (from_slot * step_count + steps[None, :]).reshape(tokens, 1)
    pick = (
        lax.broadcasted_iota(jnp.int32, (tokens, slots * step_count), 1) == comes_from
    ).astype(BF)
    acts = jnp.dot(pick, got_rows, preferred_element_type=F32).astype(BF)

    mine = [acts] + [along_y(acts, s) for s in (1, 2, 3)]
    theirs = [to_partner(block_cols) for block_cols in mine]
    where = jnp.stack([x, z, y])
    part_a, part_b = grad_parts(where, left, mine, theirs)
    part_a = total(part_a[0], *[along_x(part_a[s], s) for s in (1, 3, 2)]).astype(BF)
    part_b = total(part_b[0], *[along_z(part_b[s], s) for s in (1, 3, 2)]).astype(BF)
    sum_a = total(part_a[0], *[along_z(part_a[s], s) for s in (1, 3, 2)])
    sum_b = total(part_b[0], *[along_x(part_b[s], s) for s in (1, 3, 2)])
    piece = (jnp.concatenate([sum_a, sum_b], axis=0) / 32).astype(BF)
    grad_proj = swap_xy(piece)

    def columns(index):
        return lax.dynamic_index_in_dim(weight, index % NY, 0, keepdims=False)

    grad_blocks = [
        jnp.dot(signal, columns(y + s), preferred_element_type=F32).astype(BF) for s in range(NY)
    ]
    grad_attn = total(grad_blocks[0], *[along_y(grad_blocks[s], s) for s in (1, 3, 2)]).astype(BF)

    out_y = jnp.zeros((tokens, cotangent.shape[1]), F32)
    for s in range(NY):
        out_y = out_y + lax.dot_general(
            mine[s],
            columns(y - s + NY),
            (((1,), (1,)), ((), ())),
            preferred_element_type=F32,
        )
    return (out_y.astype(BF), grad_attn, grad_proj)


def solution(mesh):
    placed = (
        P("dp", None, "mp"),
        P("dp", None, "mp"),
        P("dp", None, "mp"),
        P("dp", None, "mp"),
        P("dp", None, "mp"),
        P("dp"),
        P("dp"),
        P("dp"),
        P("dp"),
        P("dp", "mp"),
        P("dp", "mp"),
    )
    return jax.shard_map(
        local,
        mesh=mesh,
        in_specs=placed,
        out_specs=(P("dp", "mp"), P("dp", "mp"), P("dp", "mp")),
        check_vma=False,
    )
```

```python
import functools

import jax
import jax.numpy as jnp
from jax import lax
from jax.experimental import pallas as pl
from jax.experimental.pallas import tpu as pltpu
from jax.sharding import PartitionSpec as P

HD = 128
G = 8
CAP = 8
NX, NZ, NY = 4, 4, 4
BF = jnp.bfloat16
F32 = jnp.float32


def place(x, z, c):
    return (x % NX) * 8 + (z % NZ) * 2 + c


def everywhere():
    return [(x, z, c) for x in range(NX) for z in range(NZ) for c in range(2)]


def along_x(value, shift):
    return lax.ppermute(
        value, "dp", [(place(x, z, c), place(x + shift, z, c)) for x, z, c in everywhere()]
    )


def along_z(value, shift):
    return lax.ppermute(
        value, "dp", [(place(x, z, c), place(x, z + shift, c)) for x, z, c in everywhere()]
    )


def along_y(value, shift):
    return lax.ppermute(value, "mp", [(y, (y + shift) % NY) for y in range(NY)])


def to_partner(value):
    return lax.ppermute(value, "dp", [(d, d ^ 1) for d in range(32)])


def swap_xy(value):
    pairs = [
        (place(x, z, c) * NY + y, place(y, z, c) * NY + x)
        for x, z, c in everywhere()
        for y in range(NY)
    ]
    return lax.ppermute(value, ("dp", "mp"), pairs)


def attend_kernel(
    lengths_ref, q_ref, nk_ref, nv_ref, k_ref, v_ref, out_ref, *, first
):
    rows, steps, _ = q_ref.shape
    cache = k_ref.shape[1]
    scale = HD ** (-0.5)
    base = (first + pl.program_id(0)) * rows
    q = q_ref[...].astype(F32)
    heads = [q[:, :, h * HD : (h + 1) * HD] for h in range(5)]
    heads.append(jnp.zeros_like(heads[0]))
    q = jnp.concatenate(
        [jnp.concatenate(heads[h : h + 2], axis=1) for h in (0, 2, 4)], axis=1
    ).astype(BF)
    width = q.shape[1]
    fresh = lax.dot_general(
        q.reshape(rows * width, HD),
        nk_ref[...],
        (((1,), (1,)), ((), ())),
        preferred_element_type=F32,
    )
    shape = (rows, width, rows * steps)
    col = lax.broadcasted_iota(jnp.int32, shape, 2)
    own = (col >> 2) == lax.broadcasted_iota(jnp.int32, shape, 0)
    causal = (col & 3) <= (lax.broadcasted_iota(jnp.int32, shape, 1) & 3)
    fresh = jnp.where(own & causal, fresh.reshape(shape), -jnp.inf)
    lane = lax.broadcasted_iota(jnp.int32, (width, cache), 1)
    past_weights, fresh_weights = [], []
    for r in range(rows):
        past = lax.dot_general(
            q[r], k_ref[r], (((1,), (1,)), ((), ())), preferred_element_type=F32
        )
        past = jnp.where(lane < lengths_ref[base + r], past, -jnp.inf)
        top = jnp.maximum(
            jnp.max(past, axis=-1, keepdims=True), jnp.max(fresh[r], axis=-1, keepdims=True)
        )
        past = jnp.exp((past - top) * scale)
        new = jnp.exp((fresh[r] - top) * scale)
        inverse = 1.0 / (
            jnp.sum(past, axis=-1, keepdims=True) + jnp.sum(new, axis=-1, keepdims=True)
        )
        past_weights.append((past * inverse).astype(BF))
        fresh_weights.append(new * inverse)
    fresh_weights = jnp.stack(fresh_weights, axis=0).reshape(rows * width, rows * steps)
    mixed = jnp.dot(fresh_weights.astype(BF), nv_ref[...], preferred_element_type=F32)
    mixed = mixed.reshape(rows, width, HD)
    got = [
        mixed[r] + jnp.dot(past_weights[r], v_ref[r], preferred_element_type=F32)
        for r in range(rows)
    ]
    for h in range(5):
        column = jnp.concatenate([g[h * steps : (h + 1) * steps] for g in got], axis=0)
        out_ref[:, h * HD : (h + 1) * HD] = column.astype(BF)


def attend(lengths, queries, fresh_keys, fresh_vals, key_cache, value_cache, first, count):
    rows = 8
    steps, width = queries.shape[1:]
    cache = key_cache.shape[1]
    first = first // rows
    cached = pl.BlockSpec((rows, cache, HD), lambda i, lens: (first + i, 0, 0))
    fresh = pl.BlockSpec((rows * steps, HD), lambda i, lens: (first + i, 0))
    return pl.pallas_call(
        functools.partial(attend_kernel, first=first),
        out_shape=jax.ShapeDtypeStruct((count * steps, width), BF),
        grid_spec=pltpu.PrefetchScalarGridSpec(
            num_scalar_prefetch=1,
            grid=(count // rows,),
            in_specs=[
                pl.BlockSpec((rows, steps, width), lambda i, lens: (first + i, 0, 0)),
                fresh,
                fresh,
                cached,
                cached,
            ],
            out_specs=pl.BlockSpec((rows * steps, width), lambda i, lens: (i, 0)),
        ),
        name="attend",
    )(lengths, queries, fresh_keys, fresh_vals, key_cache, value_cache)


def pack_kernel(goes_ref, facts_ref, a_ref, b_ref, out_ref):
    half = a_ref.shape[0]
    blocks = 8

    @pl.loop(0, out_ref.shape[0] // blocks)
    def _(k):
        size = blocks * 32
        slot = lax.broadcasted_iota(jnp.int32, (size, 2 * half), 0) + k * size
        chosen = (slot == goes_ref[...]).astype(F32).astype(BF)
        got = jnp.dot(chosen[:, :half], a_ref[...], preferred_element_type=F32)
        got = got + jnp.dot(chosen[:, half:], b_ref[...], preferred_element_type=F32)
        got = got.astype(BF)
        for i in range(blocks):
            out_ref[k * blocks + i, :32] = got[i * 32 : (i + 1) * 32]
            out_ref[k * blocks + i, 32:] = facts_ref[...]


def pack(goes_to, facts, first, second):
    return pl.pallas_call(
        pack_kernel,
        out_shape=jax.ShapeDtypeStruct((32, 40, first.shape[1]), BF),
        in_specs=[pl.BlockSpec(memory_space=pltpu.VMEM)] * 4,
        out_specs=pl.BlockSpec(memory_space=pltpu.VMEM),
        name="pack",
    )(goes_to, facts, first, second)


def unpack_kernel(block_ref, facts_ref, rows_ref, acts_ref, word_ref):
    tokens = acts_ref.shape[0]
    lanes = facts_ref.shape[2]
    token = lax.broadcasted_iota(jnp.int32, (tokens, lanes), 0)
    wanted = (token >> 2) + block_ref[0] * 128

    def look(k, found):
        fact = facts_ref[k].astype(F32).astype(jnp.int32)
        spot = fact[0:1] + 128 * fact[1:2]
        group = fact[2:3] * 16 + fact[3:4]
        word = group + fact[4:5] * 512 + (fact[5:6] * 4 + k * 40) * 4096
        return found + jnp.where(spot == wanted, word, 0)

    found = lax.fori_loop(0, facts_ref.shape[0], look, jnp.zeros((tokens, lanes), jnp.int32))
    found = jnp.sum(found, axis=1, keepdims=True)
    word_ref[...] = found
    total_rows = rows_ref.shape[0]
    source = (found >> 12) + (lax.broadcasted_iota(jnp.int32, (tokens, 1), 0) & 3)
    column = lax.broadcasted_iota(jnp.int32, (tokens, total_rows), 1)
    chosen = (column == source).astype(F32).astype(BF)
    acts_ref[...] = jnp.dot(chosen, rows_ref[...], preferred_element_type=F32).astype(BF)


def unpack(block, got):
    width = got.shape[2]
    return pl.pallas_call(
        unpack_kernel,
        out_shape=(
            jax.ShapeDtypeStruct((512, width), BF),
            jax.ShapeDtypeStruct((512, 1), jnp.int32),
        ),
        grid=(1,),
        in_specs=[
            pl.BlockSpec(memory_space=pltpu.SMEM),
            pl.BlockSpec((32, 8, 128), lambda i: (0, 4, 0)),
            pl.BlockSpec((32 * 40, width), lambda i: (0, 0)),
        ],
        out_specs=(
            pl.BlockSpec((512, width), lambda i: (0, 0)),
            pl.BlockSpec((512, 1), lambda i: (0, 0)),
        ),
        name="unpack",
    )(block, got, got.reshape(32 * 40, width))


def signal_kernel(facts_ref, word_ref, cot_ref, out_ref):
    tokens = out_ref.shape[0]
    lanes = facts_ref.shape[2]
    group = word_ref[...] & 511

    def add(k, sums):
        fact = facts_ref[k].astype(F32).astype(jnp.int32)
        reward = fact[4:5]
        word = reward + reward * reward * 4096
        return sums + jnp.where(fact[2:3] * 16 + fact[3:4] == group, word, 0)

    sums = lax.fori_loop(0, facts_ref.shape[0], add, jnp.zeros((tokens, lanes), jnp.int32))
    sums = jnp.sum(sums, axis=1, keepdims=True)
    centre = (sums & 4095).astype(F32) / G
    spread = (sums >> 12).astype(F32) / G - centre * centre
    reward = ((word_ref[...] >> 9) & 7).astype(F32)
    advantage = (reward - centre) / jnp.sqrt(jnp.maximum(spread, 1.0))
    out_ref[...] = (advantage * cot_ref[...].astype(F32)).astype(BF)


def weigh(got, word, cotangent):
    whole = lambda a: pl.BlockSpec(a.shape, lambda i: (0, 0))
    return pl.pallas_call(
        signal_kernel,
        out_shape=jax.ShapeDtypeStruct(cotangent.shape, BF),
        grid=(1,),
        in_specs=[
            pl.BlockSpec((32, 8, 128), lambda i: (0, 4, 0)),
            whole(word),
            whole(cotangent),
        ],
        out_specs=whole(cotangent),
        name="weigh",
    )(got, word, cotangent)


def grad_kernel(where_ref, left_ref, *refs):
    mine, theirs, (a_ref, b_ref) = refs[:4], refs[4:8], refs[8:]
    tokens = mine[0].shape[0]
    x, z, y = where_ref[0], where_ref[1], where_ref[2]
    half = left_ref.shape[0] // 2
    step = half // NZ
    for i in range(NY):
        xs = lax.rem(y - i - x + 2 * NX, NX)
        left = left_ref[...]
        got = jnp.dot(left[:, :tokens], mine[i][...], preferred_element_type=F32)
        got = got + jnp.dot(left[:, tokens:], theirs[i][...], preferred_element_type=F32)
        got = got.astype(BF)
        for k in range(NZ):
            zs = lax.rem(k - z + NZ, NZ)
            a_ref[xs, zs] = got[k * step : (k + 1) * step]
            b_ref[zs, xs] = got[half + k * step : half + (k + 1) * step]


def grad_parts(where, left, mine, theirs):
    width = mine[0].shape[1]
    step = left.shape[0] // 2 // NZ
    shape = jax.ShapeDtypeStruct((4, 4, step, width), BF)
    return pl.pallas_call(
        grad_kernel,
        out_shape=(shape, shape),
        in_specs=[pl.BlockSpec(memory_space=pltpu.SMEM)]
        + [pl.BlockSpec(memory_space=pltpu.VMEM)] * 9,
        out_specs=(
            pl.BlockSpec(memory_space=pltpu.VMEM),
            pl.BlockSpec(memory_space=pltpu.VMEM),
        ),
        name="grad_parts",
    )(where, left, *mine, *theirs)


def total(*parts):
    result = parts[0].astype(F32)
    for part in parts[1:]:
        result = result + part.astype(F32)
    return result


def local(
    queries,
    new_keys,
    new_values,
    key_cache,
    value_cache,
    lengths,
    rewards,
    group_ids,
    destination,
    out_proj,
    cotangent,
):
    row_count, step_count, feat_width = queries.shape
    tokens = row_count * step_count
    block = lax.axis_index("dp").astype(jnp.int32)
    y = lax.axis_index("mp").astype(jnp.int32)
    x, z, c = block // 8, (block // 2) % 4, block % 2

    weight_tile = swap_xy(out_proj)

    target = destination // row_count
    positions = jnp.arange(row_count, dtype=jnp.int32)
    earlier = (target[:, None] == target[None, :]) & (positions[None, :] < positions[:, None])
    rank = jnp.sum(earlier.astype(jnp.int32), axis=1)
    facts = jnp.stack(
        [destination % row_count, target, group_ids // 16, group_ids % 16, rewards, rank]
    )
    facts = jnp.pad(facts, ((0, 2), (0, feat_width - row_count))).astype(F32).astype(BF)
    steps = jnp.arange(step_count, dtype=jnp.int32)
    goes_to = ((target * CAP + rank)[:, None] * step_count + steps[None, :]).reshape(1, tokens)

    fresh_keys = new_keys.reshape(tokens, HD)
    fresh_vals = new_values.reshape(tokens, HD)
    half = row_count // 2
    caches = (fresh_keys, fresh_vals, key_cache, value_cache)
    first = attend(lengths, queries, *caches, 0, half)
    lengths, first, weight_tile = lax.optimization_barrier((lengths, first, weight_tile))
    second = attend(lengths, queries, *caches, half, half)
    weight = lax.all_gather(weight_tile, "dp", axis=0, tiled=True)
    weight = weight.reshape(NX, -1, feat_width)

    send_rows = pack(goes_to, facts, first, second)
    got_rows = lax.all_to_all(send_rows, "dp", split_axis=0, concat_axis=0, tiled=True)
    acts, word = unpack(block[None], got_rows)

    mine = [acts] + [along_y(acts, s) for s in (1, 2, 3)]
    theirs = [to_partner(block_cols) for block_cols in mine]

    signal = weigh(got_rows, word, cotangent)
    turned = signal.T.reshape(NZ, 2, 2, -1, tokens)
    sides = jnp.transpose(turned, (1, 2, 0, 3, 4)).reshape(2, -1, tokens)
    own_side = lax.dynamic_index_in_dim(sides, c, 0, keepdims=False)
    other_side = lax.dynamic_index_in_dim(sides, 1 - c, 0, keepdims=False)
    left = jnp.concatenate([own_side, to_partner(other_side)], axis=1)

    where = jnp.stack([x, z, y])
    part_a, part_b = grad_parts(where, left, mine, theirs)
    more_a = [along_x(part_a[s], s) for s in (1, 3, 2)]
    more_b = [along_z(part_b[s], s) for s in (1, 3, 2)]

    def columns(index):
        return lax.dynamic_index_in_dim(weight, index % NY, 0, keepdims=False)

    signal, _ = lax.optimization_barrier((signal, part_a))
    grad_blocks = [
        jnp.dot(signal, columns(y + s), preferred_element_type=F32).astype(BF) for s in range(NY)
    ]
    more_a, more_b, grad_blocks = lax.optimization_barrier((more_a, more_b, grad_blocks))
    more_grad = [along_y(grad_blocks[s], s) for s in (1, 3, 2)]

    part_a = total(part_a[0], *more_a).astype(BF)
    part_b = total(part_b[0], *more_b).astype(BF)
    more_a = [along_z(part_a[s], s) for s in (1, 3, 2)]
    more_b = [along_x(part_b[s], s) for s in (1, 3, 2)]

    mine, _ = lax.optimization_barrier((mine, grad_blocks))
    out_y = jnp.zeros((tokens, cotangent.shape[1]), F32)
    for s in range(NY):
        out_y = out_y + lax.dot_general(
            mine[s],
            columns(y - s + NY),
            (((1,), (1,)), ((), ())),
            preferred_element_type=F32,
        )
    out_y = out_y.astype(BF)
    more_a, more_b, out_y = lax.optimization_barrier((more_a, more_b, out_y))
    sum_a = total(part_a[0], *more_a)
    sum_b = total(part_b[0], *more_b)
    piece = (jnp.concatenate([sum_a, sum_b], axis=0) / 32).astype(BF)
    grad_proj = swap_xy(piece)
    grad_attn = total(grad_blocks[0], *more_grad).astype(BF)
    return (out_y, grad_attn, grad_proj)


def solution(mesh):
    placed = (
        P("dp", None, "mp"),
        P("dp", None, "mp"),
        P("dp", None, "mp"),
        P("dp", None, "mp"),
        P("dp", None, "mp"),
        P("dp"),
        P("dp"),
        P("dp"),
        P("dp"),
        P("dp", "mp"),
        P("dp", "mp"),
    )
    return jax.shard_map(
        local,
        mesh=mesh,
        in_specs=placed,
        out_specs=(P("dp", "mp"), P("dp", "mp"), P("dp", "mp")),
        check_vma=False,
    )
```

```python
import functools

import jax
import jax.numpy as jnp
from jax import lax
from jax.experimental import pallas as pl
from jax.experimental.pallas import tpu as pltpu
from jax.sharding import PartitionSpec as P

HD = 128
G = 8
CAP = 8
NX, NZ, NY = 4, 4, 4
BF = jnp.bfloat16
F32 = jnp.float32


def place(x, z, c):
    return (x % NX) * 8 + (z % NZ) * 2 + c


def everywhere():
    return [(x, z, c) for x in range(NX) for z in range(NZ) for c in range(2)]


def along_x(value, shift):
    return lax.ppermute(
        value, "dp", [(place(x, z, c), place(x + shift, z, c)) for x, z, c in everywhere()]
    )


def along_z(value, shift):
    return lax.ppermute(
        value, "dp", [(place(x, z, c), place(x, z + shift, c)) for x, z, c in everywhere()]
    )


def along_y(value, shift):
    return lax.ppermute(value, "mp", [(y, (y + shift) % NY) for y in range(NY)])


def to_partner(value):
    return lax.ppermute(value, "dp", [(d, d ^ 1) for d in range(32)])


def swap_xy(value):
    pairs = [
        (place(x, z, c) * NY + y, place(y, z, c) * NY + x)
        for x, z, c in everywhere()
        for y in range(NY)
    ]
    return lax.ppermute(value, ("dp", "mp"), pairs)


def attend_kernel(
    lengths_ref, q_ref, nk_ref, nv_ref, k_ref, v_ref, out_ref, *, first
):
    rows, steps, _ = q_ref.shape
    cache = k_ref.shape[1]
    scale = HD ** (-0.5)
    base = (first + pl.program_id(0)) * rows
    q = q_ref[...].astype(F32)
    heads = [q[:, :, h * HD : (h + 1) * HD] for h in range(5)]
    heads.append(jnp.zeros_like(heads[0]))
    q = jnp.concatenate(
        [jnp.concatenate(heads[h : h + 2], axis=1) for h in (0, 2, 4)], axis=1
    ).astype(BF)
    width = q.shape[1]
    fresh = lax.dot_general(
        q.reshape(rows * width, HD),
        nk_ref[...],
        (((1,), (1,)), ((), ())),
        preferred_element_type=F32,
    )
    shape = (rows, width, rows * steps)
    col = lax.broadcasted_iota(jnp.int32, shape, 2)
    own = (col >> 2) == lax.broadcasted_iota(jnp.int32, shape, 0)
    causal = (col & 3) <= (lax.broadcasted_iota(jnp.int32, shape, 1) & 3)
    fresh = jnp.where(own & causal, fresh.reshape(shape), -jnp.inf)
    lane = lax.broadcasted_iota(jnp.int32, (width, cache), 1)
    past_weights, fresh_weights = [], []
    for r in range(rows):
        past = lax.dot_general(
            q[r], k_ref[r], (((1,), (1,)), ((), ())), preferred_element_type=F32
        )
        past = jnp.where(lane < lengths_ref[base + r], past, -jnp.inf)
        top = jnp.maximum(
            jnp.max(past, axis=-1, keepdims=True), jnp.max(fresh[r], axis=-1, keepdims=True)
        )
        past = jnp.exp((past - top) * scale)
        new = jnp.exp((fresh[r] - top) * scale)
        inverse = 1.0 / (
            jnp.sum(past, axis=-1, keepdims=True) + jnp.sum(new, axis=-1, keepdims=True)
        )
        past_weights.append((past * inverse).astype(BF))
        fresh_weights.append(new * inverse)
    fresh_weights = jnp.stack(fresh_weights, axis=0).reshape(rows * width, rows * steps)
    mixed = jnp.dot(fresh_weights.astype(BF), nv_ref[...], preferred_element_type=F32)
    mixed = mixed.reshape(rows, width, HD)
    got = [
        mixed[r] + jnp.dot(past_weights[r], v_ref[r], preferred_element_type=F32)
        for r in range(rows)
    ]
    for h in range(5):
        column = jnp.concatenate([g[h * steps : (h + 1) * steps] for g in got], axis=0)
        out_ref[:, h * HD : (h + 1) * HD] = column.astype(BF)


def attend(lengths, queries, fresh_keys, fresh_vals, key_cache, value_cache, first, count):
    rows = 8
    steps, width = queries.shape[1:]
    cache = key_cache.shape[1]
    first = first // rows
    cached = pl.BlockSpec((rows, cache, HD), lambda i, lens: (first + i, 0, 0))
    fresh = pl.BlockSpec((rows * steps, HD), lambda i, lens: (first + i, 0))
    return pl.pallas_call(
        functools.partial(attend_kernel, first=first),
        out_shape=jax.ShapeDtypeStruct((count * steps, width), BF),
        grid_spec=pltpu.PrefetchScalarGridSpec(
            num_scalar_prefetch=1,
            grid=(count // rows,),
            in_specs=[
                pl.BlockSpec((rows, steps, width), lambda i, lens: (first + i, 0, 0)),
                fresh,
                fresh,
                cached,
                cached,
            ],
            out_specs=pl.BlockSpec((rows * steps, width), lambda i, lens: (i, 0)),
        ),
        name="attend",
    )(lengths, queries, fresh_keys, fresh_vals, key_cache, value_cache)


def pack_kernel(goes_ref, facts_ref, a_ref, b_ref, out_ref):
    half = a_ref.shape[0]
    blocks = 8

    @pl.loop(0, out_ref.shape[0] // blocks)
    def _(k):
        size = blocks * 32
        slot = lax.broadcasted_iota(jnp.int32, (size, 2 * half), 0) + k * size
        chosen = (slot == goes_ref[...]).astype(F32).astype(BF)
        got = jnp.dot(chosen[:, :half], a_ref[...], preferred_element_type=F32)
        got = got + jnp.dot(chosen[:, half:], b_ref[...], preferred_element_type=F32)
        got = got.astype(BF)
        for i in range(blocks):
            out_ref[k * blocks + i, :32] = got[i * 32 : (i + 1) * 32]
            out_ref[k * blocks + i, 32:] = facts_ref[...]


def pack(goes_to, facts, first, second):
    return pl.pallas_call(
        pack_kernel,
        out_shape=jax.ShapeDtypeStruct((32, 40, first.shape[1]), BF),
        in_specs=[pl.BlockSpec(memory_space=pltpu.VMEM)] * 4,
        out_specs=pl.BlockSpec(memory_space=pltpu.VMEM),
        name="pack",
    )(goes_to, facts, first, second)


def unpack_kernel(block_ref, facts_ref, rows_ref, acts_ref, word_ref):
    tokens = acts_ref.shape[0]
    lanes = facts_ref.shape[2]
    token = lax.broadcasted_iota(jnp.int32, (tokens, lanes), 0)
    wanted = (token >> 2) + block_ref[0] * 128

    def look(k, found):
        fact = facts_ref[k].astype(F32).astype(jnp.int32)
        spot = fact[0:1] + 128 * fact[1:2]
        group = fact[2:3] * 16 + fact[3:4]
        word = group + fact[4:5] * 512 + (fact[5:6] * 4 + k * 40) * 4096
        return found + jnp.where(spot == wanted, word, 0)

    found = lax.fori_loop(0, facts_ref.shape[0], look, jnp.zeros((tokens, lanes), jnp.int32))
    found = jnp.sum(found, axis=1, keepdims=True)
    word_ref[...] = found
    total_rows = rows_ref.shape[0]
    source = (found >> 12) + (lax.broadcasted_iota(jnp.int32, (tokens, 1), 0) & 3)
    column = lax.broadcasted_iota(jnp.int32, (tokens, total_rows), 1)
    chosen = (column == source).astype(F32).astype(BF)
    acts_ref[...] = jnp.dot(chosen, rows_ref[...], preferred_element_type=F32).astype(BF)


def unpack(block, got):
    width = got.shape[2]
    return pl.pallas_call(
        unpack_kernel,
        out_shape=(
            jax.ShapeDtypeStruct((512, width), BF),
            jax.ShapeDtypeStruct((512, 1), jnp.int32),
        ),
        grid=(1,),
        in_specs=[
            pl.BlockSpec(memory_space=pltpu.SMEM),
            pl.BlockSpec((32, 8, 128), lambda i: (0, 4, 0)),
            pl.BlockSpec((32 * 40, width), lambda i: (0, 0)),
        ],
        out_specs=(
            pl.BlockSpec((512, width), lambda i: (0, 0)),
            pl.BlockSpec((512, 1), lambda i: (0, 0)),
        ),
        name="unpack",
    )(block, got, got.reshape(32 * 40, width))


def signal_kernel(facts_ref, word_ref, cot_ref, out_ref):
    tokens = out_ref.shape[0]
    lanes = facts_ref.shape[2]
    group = word_ref[...] & 511

    def add(k, sums):
        fact = facts_ref[k].astype(F32).astype(jnp.int32)
        reward = fact[4:5]
        word = reward + reward * reward * 4096
        return sums + jnp.where(fact[2:3] * 16 + fact[3:4] == group, word, 0)

    sums = lax.fori_loop(0, facts_ref.shape[0], add, jnp.zeros((tokens, lanes), jnp.int32))
    sums = jnp.sum(sums, axis=1, keepdims=True)
    centre = (sums & 4095).astype(F32) / G
    spread = (sums >> 12).astype(F32) / G - centre * centre
    reward = ((word_ref[...] >> 9) & 7).astype(F32)
    advantage = (reward - centre) / jnp.sqrt(jnp.maximum(spread, 1.0))
    out_ref[...] = (advantage * cot_ref[...].astype(F32)).astype(BF)


def weigh(got, word, cotangent):
    whole = lambda a: pl.BlockSpec(a.shape, lambda i: (0, 0))
    return pl.pallas_call(
        signal_kernel,
        out_shape=jax.ShapeDtypeStruct(cotangent.shape, BF),
        grid=(1,),
        in_specs=[
            pl.BlockSpec((32, 8, 128), lambda i: (0, 4, 0)),
            whole(word),
            whole(cotangent),
        ],
        out_specs=whole(cotangent),
        name="weigh",
    )(got, word, cotangent)


def grad_kernel(where_ref, left_ref, *refs):
    mine, theirs, (a_ref, b_ref) = refs[:4], refs[4:8], refs[8:]
    tokens = mine[0].shape[0]
    x, z, y = where_ref[0], where_ref[1], where_ref[2]
    half = left_ref.shape[0] // 2
    step = half // NZ
    for i in range(NY):
        xs = lax.rem(y - i - x + 2 * NX, NX)
        left = left_ref[...]
        got = jnp.dot(left[:, :tokens], mine[i][...], preferred_element_type=F32)
        got = got + jnp.dot(left[:, tokens:], theirs[i][...], preferred_element_type=F32)
        got = got.astype(BF)
        for k in range(NZ):
            zs = lax.rem(k - z + NZ, NZ)
            a_ref[xs, zs] = got[k * step : (k + 1) * step]
            b_ref[zs, xs] = got[half + k * step : half + (k + 1) * step]


def grad_parts(where, left, mine, theirs):
    width = mine[0].shape[1]
    step = left.shape[0] // 2 // NZ
    shape = jax.ShapeDtypeStruct((4, 4, step, width), BF)
    return pl.pallas_call(
        grad_kernel,
        out_shape=(shape, shape),
        in_specs=[pl.BlockSpec(memory_space=pltpu.SMEM)]
        + [pl.BlockSpec(memory_space=pltpu.VMEM)] * 9,
        out_specs=(
            pl.BlockSpec(memory_space=pltpu.VMEM),
            pl.BlockSpec(memory_space=pltpu.VMEM),
        ),
        name="grad_parts",
    )(where, left, *mine, *theirs)


def total(*parts):
    result = parts[0].astype(F32)
    for part in parts[1:]:
        result = result + part.astype(F32)
    return result


def local(
    queries,
    new_keys,
    new_values,
    key_cache,
    value_cache,
    lengths,
    rewards,
    group_ids,
    destination,
    out_proj,
    cotangent,
):
    row_count, step_count, feat_width = queries.shape
    tokens = row_count * step_count
    block = lax.axis_index("dp").astype(jnp.int32)
    y = lax.axis_index("mp").astype(jnp.int32)
    x, z, c = block // 8, (block // 2) % 4, block % 2

    weight_tile = swap_xy(out_proj)

    target = destination // row_count
    positions = jnp.arange(row_count, dtype=jnp.int32)
    earlier = (target[:, None] == target[None, :]) & (positions[None, :] < positions[:, None])
    rank = jnp.sum(earlier.astype(jnp.int32), axis=1)
    facts = jnp.stack(
        [destination % row_count, target, group_ids // 16, group_ids % 16, rewards, rank]
    )
    facts = jnp.pad(facts, ((0, 2), (0, feat_width - row_count))).astype(F32).astype(BF)
    steps = jnp.arange(step_count, dtype=jnp.int32)
    goes_to = ((target * CAP + rank)[:, None] * step_count + steps[None, :]).reshape(1, tokens)

    fresh_keys = new_keys.reshape(tokens, HD)
    fresh_vals = new_values.reshape(tokens, HD)
    half = row_count // 2
    caches = (fresh_keys, fresh_vals, key_cache, value_cache)
    first = attend(lengths, queries, *caches, 0, half)
    second = attend(lengths, queries, *caches, half, half)
    send_rows = pack(goes_to, facts, first, second)
    got_rows = lax.all_to_all(send_rows, "dp", split_axis=0, concat_axis=0, tiled=True)
    acts, word = unpack(block[None], got_rows)

    weight_tile, _ = lax.optimization_barrier((weight_tile, got_rows))
    weight = lax.all_gather(weight_tile, "dp", axis=0, tiled=True)
    weight = weight.reshape(NX, -1, feat_width)

    mine = [acts] + [along_y(acts, s) for s in (1, 2, 3)]
    theirs = [to_partner(block_cols) for block_cols in mine]

    signal = weigh(got_rows, word, cotangent)
    turned = signal.T.reshape(NZ, 2, 2, -1, tokens)
    sides = jnp.transpose(turned, (1, 2, 0, 3, 4)).reshape(2, -1, tokens)
    own_side = lax.dynamic_index_in_dim(sides, c, 0, keepdims=False)
    other_side = lax.dynamic_index_in_dim(sides, 1 - c, 0, keepdims=False)
    left = jnp.concatenate([own_side, to_partner(other_side)], axis=1)

    where = jnp.stack([x, z, y])
    part_a, part_b = grad_parts(where, left, mine, theirs)
    more_a = [along_x(part_a[s], s) for s in (1, 3, 2)]
    more_b = [along_z(part_b[s], s) for s in (1, 3, 2)]

    def columns(index):
        return lax.dynamic_index_in_dim(weight, index % NY, 0, keepdims=False)

    signal, _ = lax.optimization_barrier((signal, part_a))
    grad_blocks = [
        jnp.dot(signal, columns(y + s), preferred_element_type=F32).astype(BF) for s in range(NY)
    ]
    more_grad = [along_y(grad_blocks[s], s) for s in (1, 3, 2)]
    more_a, more_b, more_grad = lax.optimization_barrier((more_a, more_b, more_grad))

    part_a = total(part_a[0], *more_a).astype(BF)
    part_b = total(part_b[0], *more_b).astype(BF)
    more_a = [along_z(part_a[s], s) for s in (1, 3, 2)]
    more_b = [along_x(part_b[s], s) for s in (1, 3, 2)]

    mine, _ = lax.optimization_barrier((mine, grad_blocks))
    out_y = jnp.zeros((tokens, cotangent.shape[1]), F32)
    for s in range(NY):
        out_y = out_y + lax.dot_general(
            mine[s],
            columns(y - s + NY),
            (((1,), (1,)), ((), ())),
            preferred_element_type=F32,
        )
    out_y = out_y.astype(BF)
    more_a, more_b, out_y = lax.optimization_barrier((more_a, more_b, out_y))
    sum_a = total(part_a[0], *more_a)
    sum_b = total(part_b[0], *more_b)
    piece = (jnp.concatenate([sum_a, sum_b], axis=0) / 32).astype(BF)
    grad_proj = swap_xy(piece)
    grad_attn = total(grad_blocks[0], *more_grad).astype(BF)
    return (out_y, grad_attn, grad_proj)


def solution(mesh):
    placed = (
        P("dp", None, "mp"),
        P("dp", None, "mp"),
        P("dp", None, "mp"),
        P("dp", None, "mp"),
        P("dp", None, "mp"),
        P("dp"),
        P("dp"),
        P("dp"),
        P("dp"),
        P("dp", "mp"),
        P("dp", "mp"),
    )
    return jax.shard_map(
        local,
        mesh=mesh,
        in_specs=placed,
        out_specs=(P("dp", "mp"), P("dp", "mp"), P("dp", "mp")),
        check_vma=False,
    )
```

```python
import functools

import jax
import jax.numpy as jnp
from jax import lax
from jax.experimental import pallas as pl
from jax.experimental.pallas import tpu as pltpu
from jax.sharding import PartitionSpec as P

HD = 128
G = 8
CAP = 8
NX, NZ, NY = 4, 4, 4
BF = jnp.bfloat16
F32 = jnp.float32


def place(x, z, c):
    return (x % NX) * 8 + (z % NZ) * 2 + c


def everywhere():
    return [(x, z, c) for x in range(NX) for z in range(NZ) for c in range(2)]


def along_x(value, shift):
    return lax.ppermute(
        value, "dp", [(place(x, z, c), place(x + shift, z, c)) for x, z, c in everywhere()]
    )


def along_z(value, shift):
    return lax.ppermute(
        value, "dp", [(place(x, z, c), place(x, z + shift, c)) for x, z, c in everywhere()]
    )


def along_y(value, shift):
    return lax.ppermute(value, "mp", [(y, (y + shift) % NY) for y in range(NY)])


def to_partner(value):
    return lax.ppermute(value, "dp", [(d, d ^ 1) for d in range(32)])


def swap_xy(value):
    pairs = [
        (place(x, z, c) * NY + y, place(y, z, c) * NY + x)
        for x, z, c in everywhere()
        for y in range(NY)
    ]
    return lax.ppermute(value, ("dp", "mp"), pairs)


def attend_kernel(
    lengths_ref, q_ref, nk_ref, nv_ref, k_ref, v_ref, out_ref, *, first
):
    rows, steps, _ = q_ref.shape
    cache = k_ref.shape[1]
    scale = HD ** (-0.5)
    base = (first + pl.program_id(0)) * rows
    q = q_ref[...].astype(F32)
    heads = [q[:, :, h * HD : (h + 1) * HD] for h in range(5)]
    heads.append(jnp.zeros_like(heads[0]))
    q = jnp.concatenate(
        [jnp.concatenate(heads[h : h + 2], axis=1) for h in (0, 2, 4)], axis=1
    ).astype(BF)
    width = q.shape[1]
    fresh = lax.dot_general(
        q.reshape(rows * width, HD),
        nk_ref[...],
        (((1,), (1,)), ((), ())),
        preferred_element_type=F32,
    )
    shape = (rows, width, rows * steps)
    col = lax.broadcasted_iota(jnp.int32, shape, 2)
    own = (col >> 2) == lax.broadcasted_iota(jnp.int32, shape, 0)
    causal = (col & 3) <= (lax.broadcasted_iota(jnp.int32, shape, 1) & 3)
    fresh = jnp.where(own & causal, fresh.reshape(shape), -jnp.inf)
    lane = lax.broadcasted_iota(jnp.int32, (width, cache), 1)
    past_weights, fresh_weights = [], []
    for r in range(rows):
        past = lax.dot_general(
            q[r], k_ref[r], (((1,), (1,)), ((), ())), preferred_element_type=F32
        )
        past = jnp.where(lane < lengths_ref[base + r], past, -jnp.inf)
        top = jnp.maximum(
            jnp.max(past, axis=-1, keepdims=True), jnp.max(fresh[r], axis=-1, keepdims=True)
        )
        past = jnp.exp((past - top) * scale)
        new = jnp.exp((fresh[r] - top) * scale)
        inverse = 1.0 / (
            jnp.sum(past, axis=-1, keepdims=True) + jnp.sum(new, axis=-1, keepdims=True)
        )
        past_weights.append((past * inverse).astype(BF))
        fresh_weights.append(new * inverse)
    fresh_weights = jnp.stack(fresh_weights, axis=0).reshape(rows * width, rows * steps)
    mixed = jnp.dot(fresh_weights.astype(BF), nv_ref[...], preferred_element_type=F32)
    mixed = mixed.reshape(rows, width, HD)
    got = [
        mixed[r] + jnp.dot(past_weights[r], v_ref[r], preferred_element_type=F32)
        for r in range(rows)
    ]
    for h in range(5):
        column = jnp.concatenate([g[h * steps : (h + 1) * steps] for g in got], axis=0)
        out_ref[:, h * HD : (h + 1) * HD] = column.astype(BF)


def attend(lengths, queries, fresh_keys, fresh_vals, key_cache, value_cache, first, count):
    rows = 8
    steps, width = queries.shape[1:]
    cache = key_cache.shape[1]
    first = first // rows
    cached = pl.BlockSpec((rows, cache, HD), lambda i, lens: (first + i, 0, 0))
    fresh = pl.BlockSpec((rows * steps, HD), lambda i, lens: (first + i, 0))
    return pl.pallas_call(
        functools.partial(attend_kernel, first=first),
        out_shape=jax.ShapeDtypeStruct((count * steps, width), BF),
        grid_spec=pltpu.PrefetchScalarGridSpec(
            num_scalar_prefetch=1,
            grid=(count // rows,),
            in_specs=[
                pl.BlockSpec((rows, steps, width), lambda i, lens: (first + i, 0, 0)),
                fresh,
                fresh,
                cached,
                cached,
            ],
            out_specs=pl.BlockSpec((rows * steps, width), lambda i, lens: (i, 0)),
        ),
        name="attend",
    )(lengths, queries, fresh_keys, fresh_vals, key_cache, value_cache)


def pack_kernel(goes_ref, facts_ref, a_ref, b_ref, out_ref):
    half = a_ref.shape[0]
    blocks = 8

    @pl.loop(0, out_ref.shape[0] // blocks)
    def _(k):
        size = blocks * 32
        slot = lax.broadcasted_iota(jnp.int32, (size, 2 * half), 0) + k * size
        chosen = (slot == goes_ref[...]).astype(F32).astype(BF)
        got = jnp.dot(chosen[:, :half], a_ref[...], preferred_element_type=F32)
        got = got + jnp.dot(chosen[:, half:], b_ref[...], preferred_element_type=F32)
        got = got.astype(BF)
        for i in range(blocks):
            out_ref[k * blocks + i, :32] = got[i * 32 : (i + 1) * 32]
            out_ref[k * blocks + i, 32:] = facts_ref[...]


def pack(goes_to, facts, first, second):
    return pl.pallas_call(
        pack_kernel,
        out_shape=jax.ShapeDtypeStruct((32, 40, first.shape[1]), BF),
        in_specs=[pl.BlockSpec(memory_space=pltpu.VMEM)] * 4,
        out_specs=pl.BlockSpec(memory_space=pltpu.VMEM),
        name="pack",
    )(goes_to, facts, first, second)


def unpack_kernel(block_ref, facts_ref, rows_ref, acts_ref, word_ref):
    tokens = acts_ref.shape[0]
    lanes = facts_ref.shape[2]
    token = lax.broadcasted_iota(jnp.int32, (tokens, lanes), 0)
    wanted = (token >> 2) + block_ref[0] * 128

    def look(k, found):
        fact = facts_ref[k].astype(F32).astype(jnp.int32)
        spot = fact[0:1] + 128 * fact[1:2]
        group = fact[2:3] * 16 + fact[3:4]
        word = group + fact[4:5] * 512 + (fact[5:6] * 4 + k * 40) * 4096
        return found + jnp.where(spot == wanted, word, 0)

    found = lax.fori_loop(0, facts_ref.shape[0], look, jnp.zeros((tokens, lanes), jnp.int32))
    found = jnp.sum(found, axis=1, keepdims=True)
    word_ref[...] = found
    total_rows = rows_ref.shape[0]
    source = (found >> 12) + (lax.broadcasted_iota(jnp.int32, (tokens, 1), 0) & 3)
    column = lax.broadcasted_iota(jnp.int32, (tokens, total_rows), 1)
    chosen = (column == source).astype(F32).astype(BF)
    acts_ref[...] = jnp.dot(chosen, rows_ref[...], preferred_element_type=F32).astype(BF)


def unpack(block, got):
    width = got.shape[2]
    return pl.pallas_call(
        unpack_kernel,
        out_shape=(
            jax.ShapeDtypeStruct((512, width), BF),
            jax.ShapeDtypeStruct((512, 1), jnp.int32),
        ),
        grid=(1,),
        in_specs=[
            pl.BlockSpec(memory_space=pltpu.SMEM),
            pl.BlockSpec((32, 8, 128), lambda i: (0, 4, 0)),
            pl.BlockSpec((32 * 40, width), lambda i: (0, 0)),
        ],
        out_specs=(
            pl.BlockSpec((512, width), lambda i: (0, 0)),
            pl.BlockSpec((512, 1), lambda i: (0, 0)),
        ),
        name="unpack",
    )(block, got, got.reshape(32 * 40, width))


def signal_kernel(facts_ref, word_ref, cot_ref, out_ref):
    tokens = out_ref.shape[0]
    lanes = facts_ref.shape[2]
    group = word_ref[...] & 511

    def add(k, sums):
        fact = facts_ref[k].astype(F32).astype(jnp.int32)
        reward = fact[4:5]
        word = reward + reward * reward * 4096
        return sums + jnp.where(fact[2:3] * 16 + fact[3:4] == group, word, 0)

    sums = lax.fori_loop(0, facts_ref.shape[0], add, jnp.zeros((tokens, lanes), jnp.int32))
    sums = jnp.sum(sums, axis=1, keepdims=True)
    centre = (sums & 4095).astype(F32) / G
    spread = (sums >> 12).astype(F32) / G - centre * centre
    reward = ((word_ref[...] >> 9) & 7).astype(F32)
    advantage = (reward - centre) / jnp.sqrt(jnp.maximum(spread, 1.0))
    out_ref[...] = (advantage * cot_ref[...].astype(F32)).astype(BF)


def weigh(got, word, cotangent):
    whole = lambda a: pl.BlockSpec(a.shape, lambda i: (0, 0))
    return pl.pallas_call(
        signal_kernel,
        out_shape=jax.ShapeDtypeStruct(cotangent.shape, BF),
        grid=(1,),
        in_specs=[
            pl.BlockSpec((32, 8, 128), lambda i: (0, 4, 0)),
            whole(word),
            whole(cotangent),
        ],
        out_specs=whole(cotangent),
        name="weigh",
    )(got, word, cotangent)


def grad_kernel(where_ref, left_ref, *refs):
    mine, theirs, (a_ref, b_ref) = refs[:4], refs[4:8], refs[8:]
    tokens = mine[0].shape[0]
    x, z, y = where_ref[0], where_ref[1], where_ref[2]
    half = left_ref.shape[0] // 2
    step = half // NZ
    for i in range(NY):
        xs = lax.rem(y - i - x + 2 * NX, NX)
        left = left_ref[...]
        got = jnp.dot(left[:, :tokens], mine[i][...], preferred_element_type=F32)
        got = got + jnp.dot(left[:, tokens:], theirs[i][...], preferred_element_type=F32)
        got = got.astype(BF)
        for k in range(NZ):
            zs = lax.rem(k - z + NZ, NZ)
            a_ref[xs, zs] = got[k * step : (k + 1) * step]
            b_ref[zs, xs] = got[half + k * step : half + (k + 1) * step]


def grad_parts(where, left, mine, theirs):
    width = mine[0].shape[1]
    step = left.shape[0] // 2 // NZ
    shape = jax.ShapeDtypeStruct((4, 4, step, width), BF)
    return pl.pallas_call(
        grad_kernel,
        out_shape=(shape, shape),
        in_specs=[pl.BlockSpec(memory_space=pltpu.SMEM)]
        + [pl.BlockSpec(memory_space=pltpu.VMEM)] * 9,
        out_specs=(
            pl.BlockSpec(memory_space=pltpu.VMEM),
            pl.BlockSpec(memory_space=pltpu.VMEM),
        ),
        name="grad_parts",
    )(where, left, *mine, *theirs)


def total(*parts):
    result = parts[0].astype(F32)
    for part in parts[1:]:
        result = result + part.astype(F32)
    return result


def local(
    queries,
    new_keys,
    new_values,
    key_cache,
    value_cache,
    lengths,
    rewards,
    group_ids,
    destination,
    out_proj,
    cotangent,
):
    row_count, step_count, feat_width = queries.shape
    tokens = row_count * step_count
    block = lax.axis_index("dp").astype(jnp.int32)
    y = lax.axis_index("mp").astype(jnp.int32)
    x, z, c = block // 8, (block // 2) % 4, block % 2

    weight_tile = swap_xy(out_proj)

    target = destination // row_count
    positions = jnp.arange(row_count, dtype=jnp.int32)
    earlier = (target[:, None] == target[None, :]) & (positions[None, :] < positions[:, None])
    rank = jnp.sum(earlier.astype(jnp.int32), axis=1)
    facts = jnp.stack(
        [destination % row_count, target, group_ids // 16, group_ids % 16, rewards, rank]
    )
    facts = jnp.pad(facts, ((0, 2), (0, feat_width - row_count))).astype(F32).astype(BF)
    steps = jnp.arange(step_count, dtype=jnp.int32)
    goes_to = ((target * CAP + rank)[:, None] * step_count + steps[None, :]).reshape(1, tokens)

    fresh_keys = new_keys.reshape(tokens, HD)
    fresh_vals = new_values.reshape(tokens, HD)
    half = row_count // 2
    caches = (fresh_keys, fresh_vals, key_cache, value_cache)
    first = attend(lengths, queries, *caches, 0, half)
    second = attend(lengths, queries, *caches, half, half)
    send_rows = pack(goes_to, facts, first, second)
    got_rows = lax.all_to_all(send_rows, "dp", split_axis=0, concat_axis=0, tiled=True)
    acts, word = unpack(block[None], got_rows)

    weight_tile, _ = lax.optimization_barrier((weight_tile, got_rows))
    weight = lax.all_gather(weight_tile, "dp", axis=0, tiled=True)
    weight = weight.reshape(NX, -1, feat_width)

    mine = [acts] + [along_y(acts, s) for s in (1, 2, 3)]
    theirs = [to_partner(block_cols) for block_cols in mine]

    signal = weigh(got_rows, word, cotangent)
    turned = signal.T.reshape(NZ, 2, 2, -1, tokens)
    sides = jnp.transpose(turned, (1, 2, 0, 3, 4)).reshape(2, -1, tokens)
    own_side = lax.dynamic_index_in_dim(sides, c, 0, keepdims=False)
    other_side = lax.dynamic_index_in_dim(sides, 1 - c, 0, keepdims=False)
    left = jnp.concatenate([own_side, to_partner(other_side)], axis=1)

    where = jnp.stack([x, z, y])
    part_a, part_b = grad_parts(where, left, mine, theirs)
    more_a = [along_x(part_a[s], s) for s in (1, 3, 2)]
    more_b = [along_z(part_b[s], s) for s in (1, 3, 2)]

    def columns(index):
        return lax.dynamic_index_in_dim(weight, index % NY, 0, keepdims=False)

    signal, _ = lax.optimization_barrier((signal, part_a))
    grad_blocks = [
        jnp.dot(signal, columns(y + s), preferred_element_type=F32).astype(BF) for s in range(NY)
    ]
    far_grad = along_y(grad_blocks[2], 2)
    near_grad = [along_y(grad_blocks[s], s) for s in (1, 3)]
    more_a, more_b, far_grad = lax.optimization_barrier((more_a, more_b, far_grad))

    part_a = total(part_a[0], *more_a).astype(BF)
    part_b = total(part_b[0], *more_b).astype(BF)
    more_a = [along_z(part_a[s], s) for s in (1, 3, 2)]
    more_b = [along_x(part_b[s], s) for s in (1, 3, 2)]

    mine, _ = lax.optimization_barrier((mine, grad_blocks))
    out_y = jnp.zeros((tokens, cotangent.shape[1]), F32)
    for s in range(NY):
        out_y = out_y + lax.dot_general(
            mine[s],
            columns(y - s + NY),
            (((1,), (1,)), ((), ())),
            preferred_element_type=F32,
        )
    out_y = out_y.astype(BF)
    more_a, more_b, out_y = lax.optimization_barrier((more_a, more_b, out_y))
    sum_a = total(part_a[0], *more_a)
    sum_b = total(part_b[0], *more_b)
    piece = (jnp.concatenate([sum_a, sum_b], axis=0) / 32).astype(BF)
    grad_proj = swap_xy(piece)
    grad_attn = total(grad_blocks[0], *near_grad, far_grad).astype(BF)
    return (out_y, grad_attn, grad_proj)


def solution(mesh):
    placed = (
        P("dp", None, "mp"),
        P("dp", None, "mp"),
        P("dp", None, "mp"),
        P("dp", None, "mp"),
        P("dp", None, "mp"),
        P("dp"),
        P("dp"),
        P("dp"),
        P("dp"),
        P("dp", "mp"),
        P("dp", "mp"),
    )
    return jax.shard_map(
        local,
        mesh=mesh,
        in_specs=placed,
        out_specs=(P("dp", "mp"), P("dp", "mp"), P("dp", "mp")),
        check_vma=False,
    )
```

```python
import functools

import jax
import jax.numpy as jnp
from jax import lax
from jax.experimental import pallas as pl
from jax.experimental.pallas import tpu as pltpu
from jax.sharding import PartitionSpec as P

HD = 128
G = 8
CAP = 8
NX, NZ, NY = 4, 4, 4
BF = jnp.bfloat16
F32 = jnp.float32


def place(x, z, c):
    return (x % NX) * 8 + (z % NZ) * 2 + c


def everywhere():
    return [(x, z, c) for x in range(NX) for z in range(NZ) for c in range(2)]


def along_x(value, shift):
    return lax.ppermute(
        value, "dp", [(place(x, z, c), place(x + shift, z, c)) for x, z, c in everywhere()]
    )


def along_z(value, shift):
    return lax.ppermute(
        value, "dp", [(place(x, z, c), place(x, z + shift, c)) for x, z, c in everywhere()]
    )


def along_y(value, shift):
    return lax.ppermute(value, "mp", [(y, (y + shift) % NY) for y in range(NY)])


def to_partner(value):
    return lax.ppermute(value, "dp", [(d, d ^ 1) for d in range(32)])


def swap_xy(value):
    pairs = [
        (place(x, z, c) * NY + y, place(y, z, c) * NY + x)
        for x, z, c in everywhere()
        for y in range(NY)
    ]
    return lax.ppermute(value, ("dp", "mp"), pairs)


def attend_kernel(
    lengths_ref, q_ref, nk_ref, nv_ref, k_ref, v_ref, out_ref, *, first
):
    rows, steps, _ = q_ref.shape
    cache = k_ref.shape[1]
    scale = HD ** (-0.5)
    base = (first + pl.program_id(0)) * rows
    q = q_ref[...].astype(F32)
    heads = [q[:, :, h * HD : (h + 1) * HD] for h in range(5)]
    heads.append(jnp.zeros_like(heads[0]))
    q = jnp.concatenate(
        [jnp.concatenate(heads[h : h + 2], axis=1) for h in (0, 2, 4)], axis=1
    ).astype(BF)
    width = q.shape[1]
    fresh = lax.dot_general(
        q.reshape(rows * width, HD),
        nk_ref[...],
        (((1,), (1,)), ((), ())),
        preferred_element_type=F32,
    )
    shape = (rows, width, rows * steps)
    col = lax.broadcasted_iota(jnp.int32, shape, 2)
    own = (col >> 2) == lax.broadcasted_iota(jnp.int32, shape, 0)
    causal = (col & 3) <= (lax.broadcasted_iota(jnp.int32, shape, 1) & 3)
    fresh = jnp.where(own & causal, fresh.reshape(shape), -jnp.inf)
    lane = lax.broadcasted_iota(jnp.int32, (width, cache), 1)
    past_weights, fresh_weights = [], []
    for r in range(rows):
        past = lax.dot_general(
            q[r], k_ref[r], (((1,), (1,)), ((), ())), preferred_element_type=F32
        )
        past = jnp.where(lane < lengths_ref[base + r], past, -jnp.inf)
        top = jnp.maximum(
            jnp.max(past, axis=-1, keepdims=True), jnp.max(fresh[r], axis=-1, keepdims=True)
        )
        past = jnp.exp((past - top) * scale)
        new = jnp.exp((fresh[r] - top) * scale)
        inverse = 1.0 / (
            jnp.sum(past, axis=-1, keepdims=True) + jnp.sum(new, axis=-1, keepdims=True)
        )
        past_weights.append((past * inverse).astype(BF))
        fresh_weights.append(new * inverse)
    fresh_weights = jnp.stack(fresh_weights, axis=0).reshape(rows * width, rows * steps)
    mixed = jnp.dot(fresh_weights.astype(BF), nv_ref[...], preferred_element_type=F32)
    mixed = mixed.reshape(rows, width, HD)
    got = [
        mixed[r] + jnp.dot(past_weights[r], v_ref[r], preferred_element_type=F32)
        for r in range(rows)
    ]
    for h in range(5):
        column = jnp.concatenate([g[h * steps : (h + 1) * steps] for g in got], axis=0)
        out_ref[:, h * HD : (h + 1) * HD] = column.astype(BF)


def attend(lengths, queries, fresh_keys, fresh_vals, key_cache, value_cache, first, count):
    rows = 8
    steps, width = queries.shape[1:]
    cache = key_cache.shape[1]
    first = first // rows
    cached = pl.BlockSpec((rows, cache, HD), lambda i, lens: (first + i, 0, 0))
    fresh = pl.BlockSpec((rows * steps, HD), lambda i, lens: (first + i, 0))
    return pl.pallas_call(
        functools.partial(attend_kernel, first=first),
        out_shape=jax.ShapeDtypeStruct((count * steps, width), BF),
        grid_spec=pltpu.PrefetchScalarGridSpec(
            num_scalar_prefetch=1,
            grid=(count // rows,),
            in_specs=[
                pl.BlockSpec((rows, steps, width), lambda i, lens: (first + i, 0, 0)),
                fresh,
                fresh,
                cached,
                cached,
            ],
            out_specs=pl.BlockSpec((rows * steps, width), lambda i, lens: (i, 0)),
        ),
        name="attend",
    )(lengths, queries, fresh_keys, fresh_vals, key_cache, value_cache)


def pack_kernel(goes_ref, facts_ref, a_ref, b_ref, out_ref):
    half = a_ref.shape[0]
    blocks = 8

    @pl.loop(0, out_ref.shape[0] // blocks)
    def _(k):
        size = blocks * 32
        slot = lax.broadcasted_iota(jnp.int32, (size, 2 * half), 0) + k * size
        chosen = (slot == goes_ref[...]).astype(F32).astype(BF)
        got = jnp.dot(chosen[:, :half], a_ref[...], preferred_element_type=F32)
        got = got + jnp.dot(chosen[:, half:], b_ref[...], preferred_element_type=F32)
        got = got.astype(BF)
        for i in range(blocks):
            out_ref[k * blocks + i, :32] = got[i * 32 : (i + 1) * 32]
            out_ref[k * blocks + i, 32:] = facts_ref[...]


def pack(goes_to, facts, first, second):
    return pl.pallas_call(
        pack_kernel,
        out_shape=jax.ShapeDtypeStruct((32, 40, first.shape[1]), BF),
        in_specs=[pl.BlockSpec(memory_space=pltpu.VMEM)] * 4,
        out_specs=pl.BlockSpec(memory_space=pltpu.VMEM),
        name="pack",
    )(goes_to, facts, first, second)


def unpack_kernel(block_ref, facts_ref, rows_ref, acts_ref, word_ref):
    tokens = acts_ref.shape[0]
    lanes = facts_ref.shape[2]
    token = lax.broadcasted_iota(jnp.int32, (tokens, lanes), 0)
    wanted = (token >> 2) + block_ref[0] * 128

    def look(k, found):
        fact = facts_ref[k].astype(F32).astype(jnp.int32)
        spot = fact[0:1] + 128 * fact[1:2]
        group = fact[2:3] * 16 + fact[3:4]
        word = group + fact[4:5] * 512 + (fact[5:6] * 4 + k * 40) * 4096
        return found + jnp.where(spot == wanted, word, 0)

    found = lax.fori_loop(0, facts_ref.shape[0], look, jnp.zeros((tokens, lanes), jnp.int32))
    found = jnp.sum(found, axis=1, keepdims=True)
    word_ref[...] = found
    total_rows = rows_ref.shape[0]
    source = (found >> 12) + (lax.broadcasted_iota(jnp.int32, (tokens, 1), 0) & 3)
    column = lax.broadcasted_iota(jnp.int32, (tokens, total_rows), 1)
    chosen = (column == source).astype(F32).astype(BF)
    acts_ref[...] = jnp.dot(chosen, rows_ref[...], preferred_element_type=F32).astype(BF)


def unpack(block, got):
    width = got.shape[2]
    return pl.pallas_call(
        unpack_kernel,
        out_shape=(
            jax.ShapeDtypeStruct((512, width), BF),
            jax.ShapeDtypeStruct((512, 1), jnp.int32),
        ),
        grid=(1,),
        in_specs=[
            pl.BlockSpec(memory_space=pltpu.SMEM),
            pl.BlockSpec((32, 8, 128), lambda i: (0, 4, 0)),
            pl.BlockSpec((32 * 40, width), lambda i: (0, 0)),
        ],
        out_specs=(
            pl.BlockSpec((512, width), lambda i: (0, 0)),
            pl.BlockSpec((512, 1), lambda i: (0, 0)),
        ),
        name="unpack",
    )(block, got, got.reshape(32 * 40, width))


def signal_kernel(facts_ref, word_ref, cot_ref, out_ref):
    tokens = out_ref.shape[0]
    lanes = facts_ref.shape[2]
    group = word_ref[...] & 511

    def add(k, sums):
        fact = facts_ref[k].astype(F32).astype(jnp.int32)
        reward = fact[4:5]
        word = reward + reward * reward * 4096
        return sums + jnp.where(fact[2:3] * 16 + fact[3:4] == group, word, 0)

    sums = lax.fori_loop(0, facts_ref.shape[0], add, jnp.zeros((tokens, lanes), jnp.int32))
    sums = jnp.sum(sums, axis=1, keepdims=True)
    centre = (sums & 4095).astype(F32) / G
    spread = (sums >> 12).astype(F32) / G - centre * centre
    reward = ((word_ref[...] >> 9) & 7).astype(F32)
    advantage = (reward - centre) / jnp.sqrt(jnp.maximum(spread, 1.0))
    out_ref[...] = (advantage * cot_ref[...].astype(F32)).astype(BF)


def weigh(got, word, cotangent):
    whole = lambda a: pl.BlockSpec(a.shape, lambda i: (0, 0))
    return pl.pallas_call(
        signal_kernel,
        out_shape=jax.ShapeDtypeStruct(cotangent.shape, BF),
        grid=(1,),
        in_specs=[
            pl.BlockSpec((32, 8, 128), lambda i: (0, 4, 0)),
            whole(word),
            whole(cotangent),
        ],
        out_specs=whole(cotangent),
        name="weigh",
    )(got, word, cotangent)


def grad_kernel(where_ref, left_ref, *refs, shifts, kept):
    count = len(shifts)
    mine, theirs, old = refs[:count], refs[count : 2 * count], refs[2 * count : -2]
    a_ref, b_ref = refs[-2:]
    tokens = mine[0].shape[0]
    x, z, y = where_ref[0], where_ref[1], where_ref[2]
    half = left_ref.shape[0] // 2
    step = half // NZ
    for i in kept:
        xs = lax.rem(y - i - x + 2 * NX, NX)
        a_ref[xs] = old[0][xs]
        for k in range(NZ):
            b_ref[k, xs] = old[1][k, xs]
    for n, i in enumerate(shifts):
        xs = lax.rem(y - i - x + 2 * NX, NX)
        left = left_ref[...]
        got = jnp.dot(left[:, :tokens], mine[n][...], preferred_element_type=F32)
        got = got + jnp.dot(left[:, tokens:], theirs[n][...], preferred_element_type=F32)
        got = got.astype(BF)
        for k in range(NZ):
            zs = lax.rem(k - z + NZ, NZ)
            a_ref[xs, zs] = got[k * step : (k + 1) * step]
            b_ref[zs, xs] = got[half + k * step : half + (k + 1) * step]


def grad_parts(where, left, mine, theirs, shifts, kept=(), old=()):
    width = mine[0].shape[1]
    step = left.shape[0] // 2 // NZ
    shape = jax.ShapeDtypeStruct((4, 4, step, width), BF)
    return pl.pallas_call(
        functools.partial(grad_kernel, shifts=shifts, kept=kept),
        out_shape=(shape, shape),
        in_specs=[pl.BlockSpec(memory_space=pltpu.SMEM)]
        + [pl.BlockSpec(memory_space=pltpu.VMEM)] * (1 + 2 * len(shifts) + len(old)),
        out_specs=(
            pl.BlockSpec(memory_space=pltpu.VMEM),
            pl.BlockSpec(memory_space=pltpu.VMEM),
        ),
        name="grad_parts",
    )(where, left, *mine, *theirs, *old)


def total(*parts):
    result = parts[0].astype(F32)
    for part in parts[1:]:
        result = result + part.astype(F32)
    return result


def local(
    queries,
    new_keys,
    new_values,
    key_cache,
    value_cache,
    lengths,
    rewards,
    group_ids,
    destination,
    out_proj,
    cotangent,
):
    row_count, step_count, feat_width = queries.shape
    tokens = row_count * step_count
    block = lax.axis_index("dp").astype(jnp.int32)
    y = lax.axis_index("mp").astype(jnp.int32)
    x, z, c = block // 8, (block // 2) % 4, block % 2

    weight_tile = swap_xy(out_proj)

    target = destination // row_count
    positions = jnp.arange(row_count, dtype=jnp.int32)
    earlier = (target[:, None] == target[None, :]) & (positions[None, :] < positions[:, None])
    rank = jnp.sum(earlier.astype(jnp.int32), axis=1)
    facts = jnp.stack(
        [destination % row_count, target, group_ids // 16, group_ids % 16, rewards, rank]
    )
    facts = jnp.pad(facts, ((0, 2), (0, feat_width - row_count))).astype(F32).astype(BF)
    steps = jnp.arange(step_count, dtype=jnp.int32)
    goes_to = ((target * CAP + rank)[:, None] * step_count + steps[None, :]).reshape(1, tokens)

    fresh_keys = new_keys.reshape(tokens, HD)
    fresh_vals = new_values.reshape(tokens, HD)
    half = row_count // 2
    caches = (fresh_keys, fresh_vals, key_cache, value_cache)
    first = attend(lengths, queries, *caches, 0, half)
    second = attend(lengths, queries, *caches, half, half)
    send_rows = pack(goes_to, facts, first, second)
    got_rows = lax.all_to_all(send_rows, "dp", split_axis=0, concat_axis=0, tiled=True)
    acts, word = unpack(block[None], got_rows)

    weight_tile, _ = lax.optimization_barrier((weight_tile, got_rows))
    weight = lax.all_gather(weight_tile, "dp", axis=0, tiled=True)
    weight = weight.reshape(NX, -1, feat_width)

    below, above = along_y(acts, 1), along_y(acts, 3)
    middle = tokens // 2
    far = jnp.concatenate([along_y(below[:middle], 1), along_y(above[middle:], 3)], axis=0)
    mine = [acts, below, far, above]
    theirs = [to_partner(block_cols) for block_cols in mine]

    signal = weigh(got_rows, word, cotangent)
    turned = signal.T.reshape(NZ, 2, 2, -1, tokens)
    sides = jnp.transpose(turned, (1, 2, 0, 3, 4)).reshape(2, -1, tokens)
    own_side = lax.dynamic_index_in_dim(sides, c, 0, keepdims=False)
    other_side = lax.dynamic_index_in_dim(sides, 1 - c, 0, keepdims=False)
    left = jnp.concatenate([own_side, to_partner(other_side)], axis=1)

    where = jnp.stack([x, z, y])
    near = (0, 1, 3)
    early = grad_parts(where, left, [mine[i] for i in near], [theirs[i] for i in near], near)
    part_a, part_b = grad_parts(where, left, [far], [theirs[2]], (2,), near, early)
    more_a = [along_x(part_a[s], s) for s in (1, 3, 2)]
    more_b = [along_z(part_b[s], s) for s in (1, 3, 2)]

    def columns(index):
        return lax.dynamic_index_in_dim(weight, index % NY, 0, keepdims=False)

    signal, _ = lax.optimization_barrier((signal, part_a))
    grad_blocks = [
        jnp.dot(signal, columns(y + s), preferred_element_type=F32).astype(BF) for s in range(NY)
    ]
    far_grad = along_y(grad_blocks[2], 2)
    near_grad = [along_y(grad_blocks[s], s) for s in (1, 3)]
    more_a, more_b, far_grad = lax.optimization_barrier((more_a, more_b, far_grad))

    part_a = total(part_a[0], *more_a).astype(BF)
    part_b = total(part_b[0], *more_b).astype(BF)
    more_a = [along_z(part_a[s], s) for s in (1, 3, 2)]
    more_b = [along_x(part_b[s], s) for s in (1, 3, 2)]

    mine, _ = lax.optimization_barrier((mine, grad_blocks))
    out_y = jnp.zeros((tokens, cotangent.shape[1]), F32)
    for s in range(NY):
        out_y = out_y + lax.dot_general(
            mine[s],
            columns(y - s + NY),
            (((1,), (1,)), ((), ())),
            preferred_element_type=F32,
        )
    out_y = out_y.astype(BF)
    more_a, more_b, out_y = lax.optimization_barrier((more_a, more_b, out_y))
    sum_a = total(part_a[0], *more_a)
    sum_b = total(part_b[0], *more_b)
    piece = (jnp.concatenate([sum_a, sum_b], axis=0) / 32).astype(BF)
    grad_proj = swap_xy(piece)
    grad_attn = total(grad_blocks[0], *near_grad, far_grad).astype(BF)
    return (out_y, grad_attn, grad_proj)


def solution(mesh):
    placed = (
        P("dp", None, "mp"),
        P("dp", None, "mp"),
        P("dp", None, "mp"),
        P("dp", None, "mp"),
        P("dp", None, "mp"),
        P("dp"),
        P("dp"),
        P("dp"),
        P("dp"),
        P("dp", "mp"),
        P("dp", "mp"),
    )
    return jax.shard_map(
        local,
        mesh=mesh,
        in_specs=placed,
        out_specs=(P("dp", "mp"), P("dp", "mp"), P("dp", "mp")),
        check_vma=False,
    )
```

```python
import functools

import jax
import jax.numpy as jnp
from jax import lax
from jax.experimental import pallas as pl
from jax.experimental.pallas import tpu as pltpu
from jax.sharding import PartitionSpec as P

HD = 128
G = 8
CAP = 8
NX, NZ, NY = 4, 4, 4
BF = jnp.bfloat16
F32 = jnp.float32


def place(x, z, c):
    return (x % NX) * 8 + (z % NZ) * 2 + c


def everywhere():
    return [(x, z, c) for x in range(NX) for z in range(NZ) for c in range(2)]


def along_x(value, shift):
    return lax.ppermute(
        value, "dp", [(place(x, z, c), place(x + shift, z, c)) for x, z, c in everywhere()]
    )


def along_z(value, shift):
    return lax.ppermute(
        value, "dp", [(place(x, z, c), place(x, z + shift, c)) for x, z, c in everywhere()]
    )


def along_y(value, shift):
    return lax.ppermute(value, "mp", [(y, (y + shift) % NY) for y in range(NY)])


def to_partner(value):
    return lax.ppermute(value, "dp", [(d, d ^ 1) for d in range(32)])


def swap_xy(value):
    pairs = [
        (place(x, z, c) * NY + y, place(y, z, c) * NY + x)
        for x, z, c in everywhere()
        for y in range(NY)
    ]
    return lax.ppermute(value, ("dp", "mp"), pairs)


def attend_kernel(
    lengths_ref, q_ref, nk_ref, nv_ref, k_ref, v_ref, out_ref, *, first
):
    rows, steps, _ = q_ref.shape
    cache = k_ref.shape[1]
    scale = HD ** (-0.5)
    base = (first + pl.program_id(0)) * rows
    q = q_ref[...].astype(F32)
    heads = [q[:, :, h * HD : (h + 1) * HD] for h in range(5)]
    heads.append(jnp.zeros_like(heads[0]))
    q = jnp.concatenate(
        [jnp.concatenate(heads[h : h + 2], axis=1) for h in (0, 2, 4)], axis=1
    ).astype(BF)
    width = q.shape[1]
    fresh = lax.dot_general(
        q.reshape(rows * width, HD),
        nk_ref[...],
        (((1,), (1,)), ((), ())),
        preferred_element_type=F32,
    )
    shape = (rows, width, rows * steps)
    col = lax.broadcasted_iota(jnp.int32, shape, 2)
    own = (col >> 2) == lax.broadcasted_iota(jnp.int32, shape, 0)
    causal = (col & 3) <= (lax.broadcasted_iota(jnp.int32, shape, 1) & 3)
    fresh = jnp.where(own & causal, fresh.reshape(shape), -jnp.inf)
    lane = lax.broadcasted_iota(jnp.int32, (width, cache), 1)
    past_weights, fresh_weights = [], []
    for r in range(rows):
        past = lax.dot_general(
            q[r], k_ref[r], (((1,), (1,)), ((), ())), preferred_element_type=F32
        )
        past = jnp.where(lane < lengths_ref[base + r], past, -jnp.inf)
        top = jnp.maximum(
            jnp.max(past, axis=-1, keepdims=True), jnp.max(fresh[r], axis=-1, keepdims=True)
        )
        past = jnp.exp((past - top) * scale)
        new = jnp.exp((fresh[r] - top) * scale)
        inverse = 1.0 / (
            jnp.sum(past, axis=-1, keepdims=True) + jnp.sum(new, axis=-1, keepdims=True)
        )
        past_weights.append((past * inverse).astype(BF))
        fresh_weights.append(new * inverse)
    fresh_weights = jnp.stack(fresh_weights, axis=0).reshape(rows * width, rows * steps)
    mixed = jnp.dot(fresh_weights.astype(BF), nv_ref[...], preferred_element_type=F32)
    mixed = mixed.reshape(rows, width, HD)
    got = [
        mixed[r] + jnp.dot(past_weights[r], v_ref[r], preferred_element_type=F32)
        for r in range(rows)
    ]
    for h in range(5):
        column = jnp.concatenate([g[h * steps : (h + 1) * steps] for g in got], axis=0)
        out_ref[:, h * HD : (h + 1) * HD] = column.astype(BF)


def attend(lengths, queries, fresh_keys, fresh_vals, key_cache, value_cache, first, count):
    rows = 8
    steps, width = queries.shape[1:]
    cache = key_cache.shape[1]
    first = first // rows
    cached = pl.BlockSpec((rows, cache, HD), lambda i, lens: (first + i, 0, 0))
    fresh = pl.BlockSpec((rows * steps, HD), lambda i, lens: (first + i, 0))
    return pl.pallas_call(
        functools.partial(attend_kernel, first=first),
        out_shape=jax.ShapeDtypeStruct((count * steps, width), BF),
        grid_spec=pltpu.PrefetchScalarGridSpec(
            num_scalar_prefetch=1,
            grid=(count // rows,),
            in_specs=[
                pl.BlockSpec((rows, steps, width), lambda i, lens: (first + i, 0, 0)),
                fresh,
                fresh,
                cached,
                cached,
            ],
            out_specs=pl.BlockSpec((rows * steps, width), lambda i, lens: (i, 0)),
        ),
        name="attend",
    )(lengths, queries, fresh_keys, fresh_vals, key_cache, value_cache)


def pack_kernel(goes_ref, facts_ref, a_ref, b_ref, out_ref):
    half = a_ref.shape[0]
    blocks = 8

    @pl.loop(0, out_ref.shape[0] // blocks)
    def _(k):
        size = blocks * 32
        slot = lax.broadcasted_iota(jnp.int32, (size, 2 * half), 0) + k * size
        chosen = (slot == goes_ref[...]).astype(F32).astype(BF)
        got = jnp.dot(chosen[:, :half], a_ref[...], preferred_element_type=F32)
        got = got + jnp.dot(chosen[:, half:], b_ref[...], preferred_element_type=F32)
        got = got.astype(BF)
        for i in range(blocks):
            out_ref[k * blocks + i, :32] = got[i * 32 : (i + 1) * 32]
            out_ref[k * blocks + i, 32:] = facts_ref[...]


def pack(goes_to, facts, first, second):
    return pl.pallas_call(
        pack_kernel,
        out_shape=jax.ShapeDtypeStruct((32, 40, first.shape[1]), BF),
        in_specs=[pl.BlockSpec(memory_space=pltpu.VMEM)] * 4,
        out_specs=pl.BlockSpec(memory_space=pltpu.VMEM),
        name="pack",
    )(goes_to, facts, first, second)


def unpack_kernel(block_ref, facts_ref, rows_ref, acts_ref, word_ref):
    tokens = acts_ref.shape[0]
    lanes = facts_ref.shape[2]
    token = lax.broadcasted_iota(jnp.int32, (tokens, lanes), 0)
    wanted = (token >> 2) + block_ref[0] * 128

    def look(k, found):
        fact = facts_ref[k].astype(F32).astype(jnp.int32)
        spot = fact[0:1] + 128 * fact[1:2]
        group = fact[2:3] * 16 + fact[3:4]
        word = group + fact[4:5] * 512 + (fact[5:6] * 4 + k * 40) * 4096
        return found + jnp.where(spot == wanted, word, 0)

    found = lax.fori_loop(0, facts_ref.shape[0], look, jnp.zeros((tokens, lanes), jnp.int32))
    found = jnp.sum(found, axis=1, keepdims=True)
    word_ref[...] = found
    total_rows = rows_ref.shape[0]
    source = (found >> 12) + (lax.broadcasted_iota(jnp.int32, (tokens, 1), 0) & 3)
    column = lax.broadcasted_iota(jnp.int32, (tokens, total_rows), 1)
    chosen = (column == source).astype(F32).astype(BF)
    acts_ref[...] = jnp.dot(chosen, rows_ref[...], preferred_element_type=F32).astype(BF)


def unpack(block, got):
    width = got.shape[2]
    return pl.pallas_call(
        unpack_kernel,
        out_shape=(
            jax.ShapeDtypeStruct((512, width), BF),
            jax.ShapeDtypeStruct((512, 1), jnp.int32),
        ),
        grid=(1,),
        in_specs=[
            pl.BlockSpec(memory_space=pltpu.SMEM),
            pl.BlockSpec((32, 8, 128), lambda i: (0, 4, 0)),
            pl.BlockSpec((32 * 40, width), lambda i: (0, 0)),
        ],
        out_specs=(
            pl.BlockSpec((512, width), lambda i: (0, 0)),
            pl.BlockSpec((512, 1), lambda i: (0, 0)),
        ),
        name="unpack",
    )(block, got, got.reshape(32 * 40, width))


def signal_kernel(facts_ref, word_ref, cot_ref, out_ref):
    tokens = out_ref.shape[0]
    lanes = facts_ref.shape[2]
    group = word_ref[...] & 511

    def add(k, sums):
        fact = facts_ref[k].astype(F32).astype(jnp.int32)
        reward = fact[4:5]
        word = reward + reward * reward * 4096
        return sums + jnp.where(fact[2:3] * 16 + fact[3:4] == group, word, 0)

    sums = lax.fori_loop(0, facts_ref.shape[0], add, jnp.zeros((tokens, lanes), jnp.int32))
    sums = jnp.sum(sums, axis=1, keepdims=True)
    centre = (sums & 4095).astype(F32) / G
    spread = (sums >> 12).astype(F32) / G - centre * centre
    reward = ((word_ref[...] >> 9) & 7).astype(F32)
    advantage = (reward - centre) / jnp.sqrt(jnp.maximum(spread, 1.0))
    out_ref[...] = (advantage * cot_ref[...].astype(F32)).astype(BF)


def weigh(got, word, cotangent):
    whole = lambda a: pl.BlockSpec(a.shape, lambda i: (0, 0))
    return pl.pallas_call(
        signal_kernel,
        out_shape=jax.ShapeDtypeStruct(cotangent.shape, BF),
        grid=(1,),
        in_specs=[
            pl.BlockSpec((32, 8, 128), lambda i: (0, 4, 0)),
            whole(word),
            whole(cotangent),
        ],
        out_specs=whole(cotangent),
        name="weigh",
    )(got, word, cotangent)


def grad_kernel(where_ref, left_ref, *refs, shifts, kept):
    count = len(shifts)
    mine, theirs, old = refs[:count], refs[count : 2 * count], refs[2 * count : -2]
    a_ref, b_ref = refs[-2:]
    tokens = mine[0].shape[0]
    x, z, y = where_ref[0], where_ref[1], where_ref[2]
    half = left_ref.shape[0] // 2
    step = half // NZ
    for i in kept:
        xs = lax.rem(y - i - x + 2 * NX, NX)
        a_ref[xs] = old[0][xs]
        for k in range(NZ):
            b_ref[k, xs] = old[1][k, xs]
    for n, i in enumerate(shifts):
        xs = lax.rem(y - i - x + 2 * NX, NX)
        left = left_ref[...]
        got = jnp.dot(left[:, :tokens], mine[n][...], preferred_element_type=F32)
        got = got + jnp.dot(left[:, tokens:], theirs[n][...], preferred_element_type=F32)
        got = got.astype(BF)
        for k in range(NZ):
            zs = lax.rem(k - z + NZ, NZ)
            a_ref[xs, zs] = got[k * step : (k + 1) * step]
            b_ref[zs, xs] = got[half + k * step : half + (k + 1) * step]


def grad_parts(where, left, mine, theirs, shifts, kept=(), old=()):
    width = mine[0].shape[1]
    step = left.shape[0] // 2 // NZ
    shape = jax.ShapeDtypeStruct((4, 4, step, width), BF)
    return pl.pallas_call(
        functools.partial(grad_kernel, shifts=shifts, kept=kept),
        out_shape=(shape, shape),
        in_specs=[pl.BlockSpec(memory_space=pltpu.SMEM)]
        + [pl.BlockSpec(memory_space=pltpu.VMEM)] * (1 + 2 * len(shifts) + len(old)),
        out_specs=(
            pl.BlockSpec(memory_space=pltpu.VMEM),
            pl.BlockSpec(memory_space=pltpu.VMEM),
        ),
        name="grad_parts",
    )(where, left, *mine, *theirs, *old)


def total(*parts):
    result = parts[0].astype(F32)
    for part in parts[1:]:
        result = result + part.astype(F32)
    return result


def local(
    queries,
    new_keys,
    new_values,
    key_cache,
    value_cache,
    lengths,
    rewards,
    group_ids,
    destination,
    out_proj,
    cotangent,
):
    row_count, step_count, feat_width = queries.shape
    tokens = row_count * step_count
    block = lax.axis_index("dp").astype(jnp.int32)
    y = lax.axis_index("mp").astype(jnp.int32)
    x, z, c = block // 8, (block // 2) % 4, block % 2

    weight_tile = swap_xy(out_proj)

    target = destination // row_count
    positions = jnp.arange(row_count, dtype=jnp.int32)
    earlier = (target[:, None] == target[None, :]) & (positions[None, :] < positions[:, None])
    rank = jnp.sum(earlier.astype(jnp.int32), axis=1)
    facts = jnp.stack(
        [destination % row_count, target, group_ids // 16, group_ids % 16, rewards, rank]
    )
    facts = jnp.pad(facts, ((0, 2), (0, feat_width - row_count))).astype(F32).astype(BF)
    steps = jnp.arange(step_count, dtype=jnp.int32)
    goes_to = ((target * CAP + rank)[:, None] * step_count + steps[None, :]).reshape(1, tokens)

    fresh_keys = new_keys.reshape(tokens, HD)
    fresh_vals = new_values.reshape(tokens, HD)
    half = row_count // 2
    caches = (fresh_keys, fresh_vals, key_cache, value_cache)
    first = attend(lengths, queries, *caches, 0, half)
    second = attend(lengths, queries, *caches, half, half)
    send_rows = pack(goes_to, facts, first, second)
    got_rows = lax.all_to_all(send_rows, "dp", split_axis=0, concat_axis=0, tiled=True)
    acts, word = unpack(block[None], got_rows)

    weight_tile, _ = lax.optimization_barrier((weight_tile, got_rows))
    weight = lax.all_gather(weight_tile, "dp", axis=0, tiled=True)
    weight = weight.reshape(NX, -1, feat_width)

    below, far, above = [along_y(acts, s) for s in (1, 2, 3)]
    mine = [acts, below, far, above]
    theirs = [to_partner(block_cols) for block_cols in mine]

    signal = weigh(got_rows, word, cotangent)
    turned = signal.T.reshape(NZ, 2, 2, -1, tokens)
    sides = jnp.transpose(turned, (1, 2, 0, 3, 4)).reshape(2, -1, tokens)
    own_side = lax.dynamic_index_in_dim(sides, c, 0, keepdims=False)
    other_side = lax.dynamic_index_in_dim(sides, 1 - c, 0, keepdims=False)
    left = jnp.concatenate([own_side, to_partner(other_side)], axis=1)

    where = jnp.stack([x, z, y])
    near = (0, 1, 3)
    early = grad_parts(where, left, [mine[i] for i in near], [theirs[i] for i in near], near)
    part_a, part_b = grad_parts(where, left, [far], [theirs[2]], (2,), near, early)
    more_a = [along_x(part_a[s], s) for s in (1, 3, 2)]
    more_b = [along_z(part_b[s], s) for s in (1, 3, 2)]

    def columns(index):
        return lax.dynamic_index_in_dim(weight, index % NY, 0, keepdims=False)

    signal, _ = lax.optimization_barrier((signal, part_a))
    grad_blocks = [
        jnp.dot(signal, columns(y + s), preferred_element_type=F32).astype(BF) for s in range(NY)
    ]
    far_grad = along_y(grad_blocks[2], 2)
    near_grad = [along_y(grad_blocks[s], s) for s in (1, 3)]
    more_a, more_b, far_grad = lax.optimization_barrier((more_a, more_b, far_grad))

    part_a = total(part_a[0], *more_a).astype(BF)
    part_b = total(part_b[0], *more_b).astype(BF)
    more_a = [along_z(part_a[s], s) for s in (1, 3, 2)]
    more_b = [along_x(part_b[s], s) for s in (1, 3, 2)]

    mine, _ = lax.optimization_barrier((mine, grad_blocks))
    out_y = jnp.zeros((tokens, cotangent.shape[1]), F32)
    for s in range(NY):
        out_y = out_y + lax.dot_general(
            mine[s],
            columns(y - s + NY),
            (((1,), (1,)), ((), ())),
            preferred_element_type=F32,
        )
    out_y = out_y.astype(BF)
    more_a, more_b, out_y = lax.optimization_barrier((more_a, more_b, out_y))
    sum_a = total(part_a[0], *more_a)
    sum_b = total(part_b[0], *more_b)
    piece = (jnp.concatenate([sum_a, sum_b], axis=0) / 32).astype(BF)
    grad_proj = swap_xy(piece)
    grad_attn = total(grad_blocks[0], *near_grad, far_grad).astype(BF)
    return (out_y, grad_attn, grad_proj)


def solution(mesh):
    placed = (
        P("dp", None, "mp"),
        P("dp", None, "mp"),
        P("dp", None, "mp"),
        P("dp", None, "mp"),
        P("dp", None, "mp"),
        P("dp"),
        P("dp"),
        P("dp"),
        P("dp"),
        P("dp", "mp"),
        P("dp", "mp"),
    )
    return jax.shard_map(
        local,
        mesh=mesh,
        in_specs=placed,
        out_specs=(P("dp", "mp"), P("dp", "mp"), P("dp", "mp")),
        check_vma=False,
    )
```
